512 devices in a mesh: rows: 128 (over z, x, core), half: 4 (over y).
Axes of the slice: x: 4, y: 4, z: 16, core: 2. Of those that a mesh axis runs over, the one named last changes fastest.
Arguments:
- micrograph: bfloat16 [4096, 4096], P('rows', 'half'), may hold values from -6 to 6
- box_tops: int32 [128, 4, 4, 2], replicated, may hold values from 0 to 3840, as said below
- box_live: int32 [128, 4, 4], replicated, may hold values from 0 to 1, as said below
- box_class: int32 [128, 4, 4], replicated, may hold values from 0 to 49
- box_shift: int32 [128, 4, 4, 2], P('rows', 'half'), may hold values from -8 to 8
Outputs:
- power: float32 [4, 1024, 4096], P('half', 'rows')
- class_means: float32 [50, 2, 256, 256], P(None, None, 'rows', 'half')
The draws below stay inside these ranges and needn't reach their ends.
Inputs may be any that keep to these rules, and one draw needn't show every extreme that they name: `box_tops`: the box of every slot lies inside the micrograph. A slot of box_live = 1 at index (i, j, s) has its first row among rows i * 32 to (i + 1) * 32 - 1. `box_live`: in each device's slots the live ones come first; in every draw some device has all 4 slots live.
All inputs are finite; a program needn't handle non-finite values.
Results may differ from the reference program's by a relative error of at most 0.0029.
Values may be sent and summed in bfloat16 or wider, within the bound.
A program may use at most 64 MiB of HBM per device.

```python
import jax
import jax.numpy as jnp
from jax import lax

NPIX = 4096
BOX = 256
CLASSES = 50
CAP = 4
SHIFT = 8
BANDS = 128
QUARTERS = 4
N_HALF = 4


def draw_box_tops(key, part):
    base_key = jax.random.fold_in(key, 17)
    key_rows, key_cols = jax.random.split(base_key)
    band_rows = NPIX // BANDS
    within = jax.random.randint(key_rows, (BANDS, QUARTERS, CAP), 0, band_rows)
    starts = jnp.arange(BANDS, dtype=jnp.int32)[:, None, None] * band_rows + within
    starts = jnp.minimum(starts, NPIX - BOX)
    columns = jax.random.randint(key_cols, (BANDS, QUARTERS, CAP), 0, NPIX - BOX + 1)
    return jnp.stack([starts, columns], axis=-1).astype(jnp.int32)


def draw_box_live(key, part):
    base_key = jax.random.fold_in(key, 31)
    key_one, key_three = jax.random.split(base_key, 2)
    missing = jax.random.randint(key_one, (BANDS, QUARTERS), 0, max(CAP // 2, 1) + 1)
    counts = CAP - missing
    usable = (NPIX - BOX) // (NPIX // BANDS) + 1
    chosen = jax.random.randint(key_three, (), 0, usable * QUARTERS)
    flat_index = jnp.arange(BANDS * QUARTERS, dtype=jnp.int32).reshape(BANDS, QUARTERS)
    counts = jnp.where(flat_index == chosen, CAP, counts)
    band_index = flat_index // QUARTERS
    counts = jnp.where(band_index < usable, counts, 0)
    slot_index = jnp.arange(CAP, dtype=jnp.int32)
    return (slot_index[None, None, :] < counts[:, :, None]).astype(jnp.int32)


def set_ends(array, own_key, smallest, top_value):
    longest = array.shape.index(max(array.shape))
    spots = []
    for shift in (0, 1):
        where = [jax.random.randint(jax.random.fold_in(own_key, axis), (), 0, length) for axis, length in enumerate(array.shape)]
        where[longest] = (where[longest] + shift) % array.shape[longest]
        spots.append(tuple(where))
    return array.at[spots[0]].set(smallest).at[spots[1]].set(top_value)


def levels(own_key, extent, cuts, low, top_value):
    gain, own = 1.0, jax.random.fold_in(own_key, 6)
    for axis_at, shards_of in cuts:
        steps = jnp.exp(jax.random.uniform(jax.random.fold_in(own, axis_at), (shards_of,), jnp.float32, low / len(cuts), top_value / len(cuts)))
        gain = gain * jnp.repeat(steps, extent[axis_at] // shards_of).reshape([-1 if axis == axis_at else 1 for axis in range(len(extent))])
    return gain


def normal_values(own_key, dims, width, reach, cuts=(), kind=jnp.bfloat16):
    array = jax.random.normal(own_key, dims, jnp.float32) * width
    if len(cuts) > 0:
        array = levels(own_key, dims, cuts, -0.22, 0.18) * array
    return jnp.clip(array, min=-reach, max=reach).astype(kind)


def setup_inputs(seed: int = 0) -> dict:
    streams_of = jax.random.split(jax.random.key(seed), 6)
    micrograph = normal_values(streams_of[0], (NPIX, NPIX), 1.0, 6.0, ((0, 128), (1, 4)))
    box_tops = draw_box_tops(jax.random.fold_in(streams_of[5], 71), 0)
    box_live = draw_box_live(jax.random.fold_in(streams_of[5], 71), 0)
    box_class = set_ends(jax.random.randint(streams_of[3], (BANDS, QUARTERS, CAP), 0, CLASSES), jax.random.fold_in(streams_of[3], 1), 0, CLASSES - 1).astype(jnp.int32)
    box_shift = set_ends(jax.random.randint(streams_of[4], (BANDS, QUARTERS, CAP, 2), -SHIFT, SHIFT + 1), jax.random.fold_in(streams_of[4], 1), -SHIFT, SHIFT).astype(jnp.int32)
    return dict(micrograph=micrograph, box_tops=box_tops, box_live=box_live, box_class=box_class, box_shift=box_shift)


def reference(micrograph, box_tops, box_live, box_class, box_shift):
    image_rows = micrograph.astype(jnp.float32)
    spectrum = jnp.fft.fft2(image_rows)
    real_part = jnp.real(spectrum)
    imag_part = jnp.imag(spectrum)
    power_out = (real_part * real_part + imag_part * imag_part) / (NPIX * NPIX)
    power_out = power_out.T.reshape(N_HALF, NPIX // N_HALF, NPIX)

    tops_flat = box_tops.reshape(-1, 2).astype(jnp.int32)
    shifts_flat = box_shift.reshape(-1, 2).astype(jnp.int32)
    live_flat = box_live.reshape(-1)
    labels = box_class.reshape(-1).astype(jnp.int32)
    frequency = jnp.arange(BOX, dtype=jnp.int32)

    def accumulate(totals, member):
        corner, offsets_pair, weight, label = member
        particle = lax.dynamic_slice(image_rows, (corner[0], corner[1]), (BOX, BOX))
        transformed = jnp.fft.fft2(particle) / BOX
        rotations = jnp.mod(frequency[:, None] * offsets_pair[0] + frequency[None, :] * offsets_pair[1], BOX)
        angles = (2.0 * jnp.pi / BOX) * rotations.astype(jnp.float32)
        ramp_cos = jnp.cos(angles)
        ramp_sin = jnp.sin(angles)
        trans_real = jnp.real(transformed)
        trans_imag = jnp.imag(transformed)
        out_real = trans_real * ramp_cos + trans_imag * ramp_sin
        out_imag = trans_imag * ramp_cos - trans_real * ramp_sin
        paired = jnp.stack([out_real, out_imag]).astype(jnp.bfloat16)
        paired = lax.optimization_barrier(paired).astype(jnp.float32)
        totals = totals.at[label].add(weight.astype(jnp.float32) * paired)
        return totals, None

    empty = jnp.zeros((CLASSES, 2, BOX, BOX), jnp.float32)
    totals, unused = lax.scan(accumulate, empty, (tops_flat, shifts_flat, live_flat, labels))
    classes_all = jnp.arange(CLASSES, dtype=jnp.int32)
    counts = jnp.sum((labels[None, :] == classes_all[:, None]).astype(jnp.int32) * live_flat[None, :], axis=1)
    divisor = jnp.maximum(counts, 1).astype(jnp.float32)
    class_means = totals / divisor[:, None, None, None]
    return power_out, class_means
```

```python
import functools

import jax
import jax.numpy as jnp
import numpy as np
from jax import lax
from jax.experimental import pallas as pl
from jax.experimental.pallas import tpu as pltpu
from jax.sharding import PartitionSpec as P

BOX = 256
CLASSES = 50
NPIX = 4096
NZ, NQ, NY = 16, 8, 4
NBAND = 128
REACH = 9
MESH = pl.DeviceIdType.MESH
f32 = jnp.float32
bf16 = jnp.bfloat16
VMEM = pl.BlockSpec(memory_space=pltpu.VMEM)
SMEM = pl.BlockSpec(memory_space=pltpu.SMEM)
ANY = pl.BlockSpec(memory_space=pl.ANY)


def two_parts(matrix):
    high = matrix.astype(bf16)
    return np.stack([high, (matrix - high.astype(np.float64)).astype(bf16)])


def turn(left, right, length):
    angle = 2.0 * np.pi / length * np.mod(np.multiply.outer(left, right), length)
    return np.cos(angle), np.sin(angle)


@functools.lru_cache(None)
def tables():
    out = {}
    c, s = turn(np.arange(8), np.arange(8), 8)
    eye = np.eye(32)
    out["row_one"] = two_parts(np.concatenate([np.kron(c, eye), np.kron(-s, eye)]))
    c, s = turn(np.arange(128), np.arange(512), 512)
    real = np.concatenate([c, s], axis=1)
    imag = np.concatenate([-s, c], axis=1)
    out["row_two"] = two_parts(np.stack([real, imag], axis=1).reshape(256, 1024))
    c, s = turn(np.arange(128), np.arange(128), 128)
    real = np.stack([c, s], axis=2).reshape(128, 256)
    imag = np.stack([-s, c], axis=2).reshape(128, 256)
    out["col_one"] = two_parts(np.concatenate([real, imag]))
    c, s = turn(np.arange(128), np.arange(32), NPIX)
    out["col_twist"] = np.stack([np.tile(c, (1, 4)), np.tile(s, (1, 4))]).astype(np.float32)
    c, s = turn(np.arange(32), np.arange(32), 32)
    same = np.eye(4)

    def spread(matrix):
        return np.einsum("tm,kl->tklm", matrix, same).reshape(128, 128)

    out["col_two"] = two_parts(np.block([[spread(c), spread(s)], [spread(-s), spread(c)]]))
    c, s = turn(np.arange(256), np.arange(256), 256)
    both = np.stack([c, -s]).reshape(2, NZ, NQ, 2, 256).transpose(2, 1, 0, 3, 4)
    out["box_one"] = two_parts(both.reshape(512, 256))
    c, s = turn(np.arange(32), np.arange(32), 32)
    out["box_two"] = two_parts(np.block([[c, s], [-s, c]]))
    return out


def halves(value):
    high = value.astype(bf16)
    return high, (value - high.astype(f32)).astype(bf16)


def mm(left, right):
    return lax.dot_general(left, right, (((1,), (0,)), ((), ())), preferred_element_type=f32)


def mmt(left, right):
    return lax.dot_general(left, right, (((1,), (1,)), ((), ())), preferred_element_type=f32)


def exact_product(table_ref, value, dot):
    return dot(table_ref[0], value) + dot(table_ref[1], value)


def full_product(table_ref, value, dot):
    high, low = halves(value)
    return dot(table_ref[0], high) + (dot(table_ref[1], high) + dot(table_ref[0], low))


def place():
    rows = lax.axis_index("rows")
    half = lax.axis_index("half")
    z = rows // NQ
    q = rows - z * NQ
    return rows, half, z, q, q * NY + half


def signal(barrier, rows, half):
    pl.semaphore_signal(barrier, inc=1, device_id=(rows, half), device_id_type=MESH)


def remote(src, dst, send, recv, rows, half):
    return pltpu.make_async_remote_copy(
        src_ref=src, dst_ref=dst, send_sem=send, recv_sem=recv, device_id=(rows, half), device_id_type=MESH
    )


def wait_for(ref, sem):
    pltpu.make_async_copy(ref, ref, sem).wait()


def loop(count, body, start=0):
    def step(index, carry):
        body(index)
        return carry

    lax.fori_loop(start, count, step, 0)


def gather_kernel(mic_ref, shift_ref, band_ref, table_ref, local, send, recv):
    rows, y, z, q, p = place()
    before, after = lax.rem(z + NZ - 1, NZ), lax.rem(z + 1, NZ)
    barrier = pltpu.get_barrier_semaphore()

    def greet(k):
        other = lax.rem(p + k, 32)
        signal(barrier, z * NQ + other // NY, lax.rem(other, NY))

    def greet_before(k):
        signal(barrier, before * NQ + k // NY, lax.rem(k, NY))

    loop(32, greet, 1)
    loop(32, greet_before)
    pl.semaphore_wait(barrier, 63)

    own = []
    for k in range(1, NY):
        for a in range(4):
            remote(
                mic_ref.at[:, pl.ds(256 * a, 256)], band_ref.at[NY * y + a], send.at[0], recv.at[0], rows, lax.rem(y + k, NY)
            ).start()
    for a in range(4):
        own.append(pltpu.make_async_copy(mic_ref.at[:, pl.ds(256 * a, 256)], band_ref.at[NY * y + a], local.at[a]))
    own.append(pltpu.make_async_copy(shift_ref, table_ref.at[p], local.at[4]))
    for copy in own:
        copy.start()

    def tell(k):
        other = lax.rem(p + k, 32)
        remote(shift_ref, table_ref.at[p], send.at[1], recv.at[1], z * NQ + other // NY, lax.rem(other, NY)).start()

    def tell_after(k):
        remote(shift_ref, table_ref.at[32 + p], send.at[1], recv.at[1], after * NQ + k // NY, lax.rem(k, NY)).start()

    loop(32, tell, 1)
    loop(32, tell_after)
    for copy in own:
        copy.wait()
    wait_for(band_ref.at[pl.ds(0, 12)], send.at[0])
    wait_for(band_ref.at[pl.ds(0, 12)], recv.at[0])
    wait_for(table_ref.at[pl.ds(0, 63)], send.at[1])
    wait_for(table_ref.at[pl.ds(0, 63)], recv.at[1])


def cut_kernel(where_ref, left_ref, table_ref, band_ref, boxes_ref, strip):
    q, y = where_ref[0], where_ref[1]
    lane = lax.broadcasted_iota(jnp.int32, (32, 256), 1)

    def one_band(d):
        near = q - d
        entry = jnp.where(near >= 0, near * NY + y, 32 + (near + NQ) * NY + y)
        for s in range(4):
            left = left_ref[d * 4 + s]
            block = left >> 8
            offset = left & 255
            first = band_ref[block].astype(f32)
            second = band_ref[jnp.minimum(block + 1, 15)].astype(f32)
            picked = jnp.where(lane >= offset, first, second)
            shift = (table_ref[entry, 0, 2 * s + 1] - offset) & 255
            strip[pl.ds(32 * s, 32), :] = pltpu.roll(picked, shift, 1)
        boxes_ref[:, d] = strip[...].T.reshape(32, 8, 128).astype(bf16)

    loop(REACH, one_band)


def row_kernel(band_ref, cos_ref, sin_ref, one_ref, two_ref, out_ref):
    real, imag = [], []
    for side in range(2):
        pixels = band_ref[:, side].reshape(256, 256)
        section = exact_product(one_ref, pixels, mm)
        cos = jnp.broadcast_to(cos_ref[:, 256 * side : 256 * side + 256][:, None, :], (8, 32, 256)).reshape(256, 256)
        sin = jnp.broadcast_to(sin_ref[:, 256 * side : 256 * side + 256][:, None, :], (8, 32, 256)).reshape(256, 256)
        real.append(section[:256] * cos + section[256:] * sin)
        imag.append(section[256:] * cos - section[:256] * sin)
    turned = jnp.concatenate(real + imag, axis=1)
    result = full_product(two_ref, turned, mmt).astype(bf16)
    out_ref[0] = result[:, :128]
    out_ref[1] = result[:, 128:]


def spread_kernel(freq_ref, boxes_ref, freq_out, boxes_out, local, send, recv):
    rows, y, z, q, p = place()
    before, after = lax.rem(z + NZ - 1, NZ), lax.rem(z + 1, NZ)
    barrier = pltpu.get_barrier_semaphore()

    def greet_rows(k):
        signal(barrier, lax.rem(rows + k, NBAND), y)

    def greet(k):
        other = lax.rem(p + k, 32)
        signal(barrier, z * NQ + other // NY, lax.rem(other, NY))

    def greet_after(k):
        signal(barrier, after * NQ + k // NY, lax.rem(k, NY))

    loop(NBAND, greet_rows, 1)
    loop(32, greet, 1)
    loop(32, greet_after)
    pl.semaphore_wait(barrier, NBAND - 1 + 63)

    def send_rows(k):
        other = lax.rem(rows + k, NBAND)
        remote(freq_ref.at[:, other], freq_out.at[:, rows], send.at[0], recv.at[0], other, y).start()

    here = p * REACH
    own_freq = pltpu.make_async_copy(freq_ref.at[:, rows], freq_out.at[:, rows], local.at[0])
    own_freq.start()

    for level in range(NQ):

        @pl.when(q == level)
        def _():
            near, far = level + 1, REACH - 1 - level

            def send_far(k):
                remote(
                    boxes_ref.at[pl.ds(k * REACH + near, far)],
                    boxes_out.at[pl.ds(here + near, far)],
                    send.at[2],
                    recv.at[2],
                    before * NQ + k // NY,
                    lax.rem(k, NY),
                ).start()

            def send_near(k):
                other = lax.rem(p + k, 32)
                remote(
                    boxes_ref.at[pl.ds(other * REACH, near)],
                    boxes_out.at[pl.ds(here, near)],
                    send.at[1],
                    recv.at[1],
                    z * NQ + other // NY,
                    lax.rem(other, NY),
                ).start()

            loop(32, send_far)
            loop(32, send_near, 1)
            own = pltpu.make_async_copy(boxes_ref.at[pl.ds(here, near)], boxes_out.at[pl.ds(here, near)], local.at[1])
            own.start()
            loop(NBAND, send_rows, 1)
            own.wait()
            wait_for(boxes_ref.at[pl.ds(0, 32 * far)], send.at[2])
            wait_for(boxes_ref.at[pl.ds(0, 31 * near)], send.at[1])
            wait_for(boxes_out.at[pl.ds(0, 144 - near)], recv.at[1])

    wait_for(boxes_out.at[pl.ds(0, 144)], recv.at[2])
    own_freq.wait()
    wait_for(freq_out.at[:, pl.ds(0, NBAND - 1)], send.at[0])
    wait_for(freq_out.at[:, pl.ds(0, NBAND - 1)], recv.at[0])


def class_kernel(top_ref, label_ref, table_ref, boxes_ref, one_ref, out_ref, acc):
    acc[...] = jnp.zeros_like(acc)
    lane = lax.broadcasted_iota(jnp.int32, (8, 128), 1)
    group = lane >> 5

    def one_home(home):
        q0 = home >> 2
        j = home & 3
        spun = []
        for d in range(REACH):
            piece = boxes_ref[(((q0 + d) & 7) * NY + j) * REACH + d].astype(f32)
            spun.append([piece] + [pltpu.roll(piece, 32 * turns, 1) for turns in range(1, 4)])

        def joined(first, s):
            value = spun[first][(0 - s) % 4]
            for dd in range(1, 4):
                value = jnp.where(group == dd, spun[first + dd][(dd - s) % 4], value)
            return value

        for s in range(4):
            slot = home * 4 + s
            top = top_ref[slot]
            shift = (table_ref[home, 0, 2 * s] - top) & 255
            low = jnp.where(lane >= top, joined(0, s), spun[8][(0 - s) % 4])
            box = pltpu.roll(jnp.concatenate([low, joined(4, s)], axis=1), shift, 1)
            label = label_ref[slot]
            acc[label] = acc[label] + box

    loop(32, one_home)
    main = full_product(one_ref, acc[0:48].reshape(384, 256), mmt).astype(bf16)
    for q in range(NQ):
        for t in range(3):
            out_ref[3 * q + t] = main[64 * q : 64 * q + 64, 128 * t : 128 * t + 128]
    rest = full_product(one_ref, acc[48:50].reshape(16, 256), mmt)
    rest = jnp.concatenate([rest[64 * q : 64 * q + 64] for q in range(NQ)], axis=1)
    out_ref[24] = rest.astype(bf16)


def sum_kernel(send_ref, got_ref, landed, sums, local, send, recv):
    rows, y, z, q, p = place()
    barrier = pltpu.get_barrier_semaphore()

    def greet_z(k):
        signal(barrier, lax.rem(z + k, NZ) * NQ + q, y)

    def greet(k):
        other = lax.rem(p + k, 32)
        signal(barrier, z * NQ + other // NY, lax.rem(other, NY))

    loop(NZ, greet_z, 1)
    loop(32, greet, 1)
    pl.semaphore_wait(barrier, 15 + 31)

    def send_z(k):
        other = lax.rem(z + k, NZ)
        remote(send_ref.at[:, other], landed.at[:, z], send.at[0], recv.at[0], other * NQ + q, y).start()

    loop(NZ, send_z, 1)
    own = pltpu.make_async_copy(send_ref.at[:, z], landed.at[:, z], local.at[0])
    own.start()
    own.wait()
    wait_for(landed.at[:, pl.ds(0, 15)], send.at[0])
    wait_for(landed.at[:, pl.ds(0, 15)], recv.at[0])
    for block in range(25):
        sums[block] = jnp.sum(landed[block].astype(f32), axis=0)

    def send_plane(k):
        other = lax.rem(p + k, 32)
        there = other // NY
        target = (z * NQ + there, lax.rem(other, NY))
        remote(sums.at[pl.ds(3 * there, 3)], got_ref.at[p, pl.ds(0, 3)], send.at[1], recv.at[1], *target).start()
        remote(sums.at[24], got_ref.at[p, 3], send.at[2], recv.at[2], *target).start()

    loop(32, send_plane, 1)
    mine = [
        pltpu.make_async_copy(sums.at[pl.ds(3 * q, 3)], got_ref.at[p, pl.ds(0, 3)], local.at[1]),
        pltpu.make_async_copy(sums.at[24], got_ref.at[p, 3], local.at[2]),
    ]
    for copy in mine:
        copy.start()
    for copy in mine:
        copy.wait()
    for index, count in ((1, 3), (2, 1)):
        wait_for(got_ref.at[pl.ds(0, 31), pl.ds(0, count)], send.at[index])
        wait_for(got_ref.at[pl.ds(0, 31), pl.ds(0, count)], recv.at[index])


def mean_kernel(where_ref, sums_ref, cos_ref, sin_ref, inverse_ref, two_ref, out_ref):
    q = where_ref[0]
    pieces = []
    for t in range(4):
        for a in range(2):
            pieces.append(jnp.concatenate([sums_ref[:, 4 * t + a, :], sums_ref[:, 4 * t + 2 + a, :]], axis=0))
    section = full_product(two_ref, jnp.concatenate(pieces, axis=1), mm)
    cos, sin = cos_ref[...], sin_ref[...]
    pattern = lax.broadcasted_iota(jnp.int32, (16, 128), 1) >> 3
    kind = lax.broadcasted_iota(jnp.int32, (16, 128), 0)
    for t in range(4):
        pick = (pattern == (kind if t < 3 else kind + 2 * q)).astype(bf16)
        for a in range(2):
            at = 128 * (2 * t + a)
            real = jnp.concatenate([section[:32, at : at + 128]] * 2, axis=0)
            imag = jnp.concatenate([section[32:, at : at + 128]] * 2, axis=0)
            for part, value in enumerate((real * cos + imag * sin, imag * cos - real * sin)):
                high, low = halves(value)
                total = mmt(pick, high) + mmt(pick, low)
                if t < 3:
                    out_ref[16 * t : 16 * t + 16, part, a, :] = total * inverse_ref[16 * t : 16 * t + 16]
                else:
                    out_ref[48:50, part, a, :] = total[:2] * inverse_ref[48:50]


def column_kernel(freq_ref, one_ref, twist_ref, two_ref, out_ref):
    cos, sin = twist_ref[0], twist_ref[1]
    for h in range(2):
        section = exact_product(one_ref, freq_ref[h], mm)
        real = section[:128] * cos + section[128:] * sin
        imag = section[128:] * cos - section[:128] * sin
        result = full_product(two_ref, jnp.concatenate([real, imag], axis=1), mmt)
        power = (result[:128] * result[:128] + result[128:] * result[128:]) * (1.0 / (NPIX * NPIX))
        for tau in range(32):
            out_ref[0, 4 * h : 4 * h + 4, 128 * tau : 128 * tau + 128] = power[4 * tau : 4 * tau + 4]


def call(kernel, outs, ins, out_specs, scratch=(), collective=None, name=None):
    params = dict(has_side_effects=True, collective_id=collective) if collective is not None else {}
    return pl.pallas_call(
        kernel,
        out_shape=outs,
        in_specs=ins,
        out_specs=out_specs,
        scratch_shapes=list(scratch),
        compiler_params=pltpu.CompilerParams(**params),
        name=name,
    )


def shape(*dims, dtype=bf16):
    return jax.ShapeDtypeStruct(dims, dtype)


def sems(count):
    return pltpu.SemaphoreType.DMA((count,))


def per_device(micrograph, box_tops, box_live, box_class, box_shift):
    consts = {name: jnp.asarray(value) for name, value in tables().items()}
    rows = lax.axis_index("rows")
    y = lax.axis_index("half")
    z = rows // NQ
    q = rows - z * NQ
    where = jnp.stack([q, y]).astype(jnp.int32)

    shifts = jnp.pad(box_shift.reshape(1, 8), ((0, 0), (0, 120)))
    band, table = call(
        gather_kernel,
        (shape(16, 32, 256), shape(64, 1, 128, dtype=jnp.int32)),
        [ANY, VMEM],
        (VMEM, VMEM),
        (sems(5), sems(2), sems(2)),
        collective=0,
        name="gather",
    )(micrograph, shifts)

    homes = jnp.mod(rows - jnp.arange(REACH, dtype=jnp.int32), NBAND)
    lefts = box_tops[homes, y, :, 1].reshape(-1)
    boxes = call(
        cut_kernel,
        shape(32, REACH, 8, 128),
        [SMEM, SMEM, SMEM, VMEM],
        VMEM,
        (pltpu.VMEM((128, 256), f32),),
        name="cut",
    )(where, lefts, table, band)

    octant = jnp.arange(8, dtype=jnp.int32)[:, None]
    column = jnp.arange(512, dtype=jnp.int32)[None, :]
    angles = (2.0 * np.pi / NPIX) * jnp.mod(column * (octant + 1024 * y), NPIX).astype(f32)
    freq = call(row_kernel, shape(2, 256, 128), [VMEM] * 5, VMEM, name="row")(
        band.reshape(8, 2, 32, 256), jnp.cos(angles), jnp.sin(angles), consts["row_one"], consts["row_two"]
    )

    freq, boxes = call(
        spread_kernel,
        (shape(2, NBAND, 2, 128), shape(32 * REACH, 8, 128)),
        [VMEM, VMEM],
        (VMEM, VMEM),
        (sems(2), sems(3), sems(3)),
        collective=1,
        name="spread",
    )(freq.reshape(2, NBAND, 2, 128), boxes.reshape(32 * REACH, 8, 128))

    plane_tops = lax.dynamic_slice_in_dim(box_tops[..., 0], z * NQ, NQ, 0)
    band_tops = (z * NQ + jnp.arange(NQ, dtype=jnp.int32)) * 32
    tops = (plane_tops - band_tops[:, None, None]).reshape(-1)
    plane_class = lax.dynamic_slice_in_dim(jnp.where(box_live == 1, box_class, CLASSES), z * NQ, NQ, 0)
    labels = plane_class.reshape(-1)
    to_z = call(
        class_kernel,
        shape(25, 64, 128),
        [SMEM, SMEM, SMEM, VMEM, VMEM],
        VMEM,
        (pltpu.VMEM((CLASSES + 1, 8, 256), f32),),
        name="classes",
    )(tops, labels, table, boxes, consts["box_one"])

    sums = call(
        sum_kernel,
        shape(32, 4, 4, 128, dtype=f32),
        [VMEM],
        VMEM,
        (pltpu.VMEM((25, NZ, 4, 128), bf16), pltpu.VMEM((25, 4, 128), f32), sems(3), sems(3), sems(3)),
        collective=2,
        name="sums",
    )(to_z.reshape(25, NZ, 4, 128))

    power = call(column_kernel, shape(1, 8, NPIX, dtype=f32), [VMEM] * 4, VMEM, name="column")(
        freq.reshape(2, 256, 128), consts["col_one"], consts["col_twist"], consts["col_two"]
    )

    kinds = jnp.arange(CLASSES, dtype=jnp.int32)[:, None, None, None]
    counts = jnp.sum(((box_class[None] == kinds) & (box_live[None] == 1)).astype(jnp.int32), axis=(1, 2, 3))
    inverse = (1.0 / (BOX * jnp.maximum(counts, 1).astype(f32)))[:, None]
    beta = jnp.arange(64, dtype=jnp.int32)[:, None] + 64 * y
    inner = jnp.arange(128, dtype=jnp.int32)[None, :] & 7
    angles = (2.0 * np.pi / BOX) * jnp.mod(beta * inner, BOX).astype(f32)
    means = call(
        mean_kernel, shape(CLASSES, 2, 2, 64, dtype=f32), [SMEM] + [VMEM] * 5, VMEM, name="means"
    )(where, sums.reshape(32, 16, 128), jnp.cos(angles), jnp.sin(angles), inverse, consts["box_two"])
    return power, means


def solution(mesh):
    in_specs = (P("rows", "half"), P(), P(), P(), P("rows", "half", None, None))
    out_specs = (P("half", "rows", None), P(None, None, "rows", "half"))
    return jax.shard_map(per_device, mesh=mesh, in_specs=in_specs, out_specs=out_specs, check_vma=False)
```

```python
import functools

import jax
import jax.numpy as jnp
import numpy as np
from jax import lax
from jax.experimental import pallas as pl
from jax.experimental.pallas import tpu as pltpu
from jax.sharding import PartitionSpec as P

BOX = 256
CLASSES = 50
NPIX = 4096
NZ, NQ, NY = 16, 8, 4
NBAND = 128
REACH = 9
MESH = pl.DeviceIdType.MESH
f32 = jnp.float32
bf16 = jnp.bfloat16
VMEM = pl.BlockSpec(memory_space=pltpu.VMEM)
SMEM = pl.BlockSpec(memory_space=pltpu.SMEM)
ANY = pl.BlockSpec(memory_space=pl.ANY)


def two_parts(matrix):
    high = matrix.astype(bf16)
    return np.stack([high, (matrix - high.astype(np.float64)).astype(bf16)])


def turn(left, right, length):
    angle = 2.0 * np.pi / length * np.mod(np.multiply.outer(left, right), length)
    return np.cos(angle), np.sin(angle)


@functools.lru_cache(None)
def tables():
    out = {}
    c, s = turn(np.arange(8), np.arange(8), 8)
    eye = np.eye(32)
    out["row_one"] = two_parts(np.concatenate([np.kron(c, eye), np.kron(-s, eye)]))
    angle = np.arange(8)[None] + 1024 * np.arange(4)[:, None]
    c, s = turn(angle, np.arange(512), NPIX)
    out["row_twist"] = np.stack([c, s], axis=1).astype(np.float32)
    c, s = turn(np.arange(128), np.arange(512), 512)
    real = np.concatenate([c, s], axis=1)
    imag = np.concatenate([-s, c], axis=1)
    out["row_two"] = two_parts(np.stack([real, imag], axis=1).reshape(256, 1024))
    c, s = turn(np.arange(128), np.arange(128), 128)
    real = np.stack([c, s], axis=2)
    imag = np.stack([-s, c], axis=2)
    both = np.concatenate([real, imag]).reshape(256, NZ, NQ, 2).transpose(0, 2, 1, 3)
    out["col_one"] = two_parts(both.reshape(256, 256))
    c, s = turn(np.arange(128), np.arange(32), NPIX)
    out["col_twist"] = np.stack([np.tile(c, (1, 4)), np.tile(s, (1, 4))]).astype(np.float32)
    c, s = turn(np.arange(32), np.arange(32), 32)
    same = np.eye(4)

    def spread(matrix):
        return np.einsum("tm,kl->tklm", matrix, same).reshape(128, 128)

    out["col_two"] = two_parts(np.block([[spread(c), spread(s)], [spread(-s), spread(c)]]))
    c, s = turn(np.arange(256), np.arange(256), 256)
    both = np.stack([c, -s]).reshape(2, NZ, NQ, 2, 256).transpose(2, 1, 0, 3, 4)
    out["box_one"] = two_parts(both.reshape(512, 256))
    c, s = turn(np.arange(32), np.arange(32), 32)
    out["box_two"] = two_parts(np.block([[c, s], [-s, c]]))
    lanes = np.concatenate([np.arange(384) // 48, (np.arange(128) >> 1) & 7])
    c, s = turn(np.arange(64), lanes, 256)
    out["box_twist"] = np.stack([c, s]).astype(np.float32)
    c, s = turn(np.arange(4), lanes, 4)
    out["box_quarter"] = np.stack([c, s], axis=1).reshape(4, 2, 512).astype(np.float32)
    return out


def halves(value):
    high = value.astype(bf16)
    return high, (value - high.astype(f32)).astype(bf16)


def mm(left, right):
    return lax.dot_general(left, right, (((1,), (0,)), ((), ())), preferred_element_type=f32)


def mmt(left, right):
    return lax.dot_general(left, right, (((1,), (1,)), ((), ())), preferred_element_type=f32)


def exact_product(table_ref, value, dot):
    return dot(table_ref[0], value) + dot(table_ref[1], value)


def full_product(table_ref, value, dot):
    high, low = halves(value)
    return dot(table_ref[0], high) + (dot(table_ref[1], high) + dot(table_ref[0], low))


def place():
    rows = lax.axis_index("rows")
    half = lax.axis_index("half")
    z = rows // NQ
    q = rows - z * NQ
    return rows, half, z, q, q * NY + half


def signal(barrier, rows, half):
    pl.semaphore_signal(barrier, inc=1, device_id=(rows, half), device_id_type=MESH)


def remote(src, dst, send, recv, rows, half):
    return pltpu.make_async_remote_copy(
        src_ref=src, dst_ref=dst, send_sem=send, recv_sem=recv, device_id=(rows, half), device_id_type=MESH
    )


def wait_for(ref, sem):
    pltpu.make_async_copy(ref, ref, sem).wait()


def loop(count, body, start=0):
    def step(index, carry):
        body(index)
        return carry

    lax.fori_loop(start, count, step, 0)


def signal_plane(barrier, z, p):
    def greet(k):
        other = lax.rem(p + k, 32)
        signal(barrier, z * NQ + other // NY, lax.rem(other, NY))

    loop(32, greet, 1)


def gather_kernel(mic_ref, shift_ref, band_ref, table_ref, local, send, recv):
    rows, y, z, q, p = place()
    before, after = lax.rem(z + NZ - 1, NZ), lax.rem(z + 1, NZ)
    own = []
    for a in range(4):
        own.append(pltpu.make_async_copy(mic_ref.at[:, pl.ds(256 * a, 256)], band_ref.at[NY * y + a], local.at[a]))
    own.append(pltpu.make_async_copy(shift_ref, table_ref.at[p], local.at[4]))
    for copy in own:
        copy.start()
    barrier = pltpu.get_barrier_semaphore()
    signal_plane(barrier, z, p)
    for k in range(NQ):
        signal(barrier, before * NQ + k, y)
    for copy in own:
        copy.wait()
    pl.semaphore_wait(barrier, 31 + NQ)

    mine = band_ref.at[pl.ds(NY * y, 4)]
    for k in range(1, NY):
        remote(mine, mine, send.at[0], recv.at[0], rows, lax.rem(y + k, NY)).start()
    for k in range(NQ):
        remote(table_ref.at[p], table_ref.at[32 + q], send.at[1], recv.at[1], after * NQ + k, y).start()

    def tell(k):
        other = lax.rem(p + k, 32)
        remote(
            table_ref.at[p], table_ref.at[p], send.at[1], recv.at[1], z * NQ + other // NY, lax.rem(other, NY)
        ).start()

    loop(32, tell, 1)
    wait_for(band_ref.at[pl.ds(0, 12)], send.at[0])
    wait_for(table_ref.at[pl.ds(0, 31 + NQ)], send.at[1])
    wait_for(band_ref.at[pl.ds(0, 12)], recv.at[0])
    wait_for(table_ref.at[pl.ds(0, 31 + NQ)], recv.at[1])


def spread_kernel(
    code_ref, table_ref, band_ref, twist_ref, one_hbm, two_hbm, freq_out, boxes_out,
    one_ref, two_ref, strip, boxes, freq, local, send, recv,
):
    rows, y, z, q, p = place()
    before, after = lax.rem(z + NZ - 1, NZ), lax.rem(z + 1, NZ)
    barrier = pltpu.get_barrier_semaphore()
    load_one = pltpu.make_async_copy(one_hbm, one_ref, local.at[0])
    load_two = pltpu.make_async_copy(two_hbm, two_ref, local.at[1])
    load_one.start()
    load_two.start()

    def greet_z(k):
        signal(barrier, lax.rem(z + k, NZ) * NQ + q, y)

    def greet_after(k):
        signal(barrier, after * NQ + k // NY, lax.rem(k, NY))

    loop(NZ, greet_z, 1)
    signal_plane(barrier, z, p)
    loop(32, greet_after)

    lane = lax.broadcasted_iota(jnp.int32, (32, 256), 1)

    def one_band(d):
        near = q - d
        entry = jnp.where(near >= 0, near * NY + y, 32 + near + NQ)
        home = lax.rem(rows - d + NBAND, NBAND)
        for s in range(4):
            left = (code_ref[home // NQ, lax.rem(home, NQ) * 16 + y * 4 + s] >> 12) & 4095
            block = left >> 8
            offset = left & 255
            first = band_ref[block].astype(f32)
            second = band_ref[jnp.minimum(block + 1, 15)].astype(f32)
            picked = jnp.where(lane >= offset, first, second)
            shift = (table_ref[entry, 0, 2 * s + 1] - offset) & 255
            strip[pl.ds(32 * s, 32), :] = pltpu.roll(picked, shift, 1)
        boxes[:, d] = strip[...].T.reshape(32, 8, 128).astype(bf16)

    loop(REACH, one_band)
    pl.semaphore_wait(barrier, 15 + 63)

    here = p
    for level in range(NQ):

        @pl.when(q == level)
        def _():
            near, far = level + 1, REACH - 1 - level

            def send_far(k):
                remote(
                    boxes.at[k, pl.ds(near, far)], boxes_out.at[pl.ds(here * REACH + near, far)],
                    send.at[2], recv.at[2], before * NQ + k // NY, lax.rem(k, NY),
                ).start()

            def send_near(k):
                other = lax.rem(p + k, 32)
                remote(
                    boxes.at[other, pl.ds(0, near)], boxes_out.at[pl.ds(here * REACH, near)],
                    send.at[1], recv.at[1], z * NQ + other // NY, lax.rem(other, NY),
                ).start()

            loop(32, send_far)
            loop(32, send_near, 1)
            pltpu.make_async_copy(boxes.at[here, pl.ds(0, near)], boxes_out.at[pl.ds(here * REACH, near)], local.at[2]).start()

    load_one.wait()
    load_two.wait()
    real, imag = [], []
    cos_all, sin_all = twist_ref[y, 0], twist_ref[y, 1]
    for side in range(2):
        pixels = band_ref[:, :].reshape(8, 2, 32, 256)[:, side].reshape(256, 256)
        section = exact_product(one_ref, pixels, mm)
        cos = jnp.broadcast_to(cos_all[:, 256 * side : 256 * side + 256][:, None, :], (8, 32, 256)).reshape(256, 256)
        sin = jnp.broadcast_to(sin_all[:, 256 * side : 256 * side + 256][:, None, :], (8, 32, 256)).reshape(256, 256)
        real.append(section[:256] * cos + section[256:] * sin)
        imag.append(section[256:] * cos - section[:256] * sin)
    turned = jnp.concatenate(real + imag, axis=1)
    result = full_product(two_ref, turned, mmt).astype(bf16)
    freq[0] = result[:, :128]
    freq[1] = result[:, 128:]

    def send_z(k):
        other = lax.rem(z + k, NZ)
        remote(
            freq.at[:, pl.ds(16 * other, 16)], freq_out.at[:, z], send.at[0], recv.at[0], other * NQ + q, y
        ).start()

    loop(NZ, send_z, 1)
    own = pltpu.make_async_copy(freq.at[:, pl.ds(16 * z, 16)], freq_out.at[:, z], local.at[3])
    own.start()

    for level in range(NQ):

        @pl.when(q == level)
        def _():
            near, far = level + 1, REACH - 1 - level
            wait_for(boxes.at[0, pl.ds(0, near)], local.at[2])
            wait_for(boxes.at[pl.ds(0, 32), pl.ds(0, far)], send.at[2])
            wait_for(boxes.at[pl.ds(0, 31), pl.ds(0, near)], send.at[1])
            wait_for(whole_pieces(boxes_out, 144 - near), recv.at[1])

    wait_for(whole_pieces(boxes_out, 144), recv.at[2])
    own.wait()
    wait_for(freq_out.at[:, pl.ds(0, 15)], send.at[0])
    wait_for(freq_out.at[:, pl.ds(0, 15)], recv.at[0])


def sum_kernel(
    code_ref, table_ref, labels_ref, boxes_ref, freq_ref, one_hbm, two_ref, twist_ref, quarter_ref, col_one_hbm, col_twist_ref,
    col_two_hbm, power_ref, means_ref, one_ref, col_one_ref, col_two_ref, held, to_z, landed, sums, got, freq, local, send, recv,
):
    rows, y, z, q, p = place()
    barrier = pltpu.get_barrier_semaphore()
    loads = [
        pltpu.make_async_copy(one_hbm, one_ref, local.at[4]),
        pltpu.make_async_copy(col_one_hbm, col_one_ref, local.at[5]),
        pltpu.make_async_copy(col_two_hbm, col_two_ref, local.at[6]),
    ]
    for load in loads:
        load.start()

    def greet_z(k):
        signal(barrier, lax.rem(z + k, NZ) * NQ + q, y)

    loop(NZ, greet_z, 1)
    signal_plane(barrier, z, p)

    lane = lax.broadcasted_iota(jnp.int32, (8, 128), 1)
    group = lane >> 5

    def one_home(home):
        q0 = home >> 2
        j = home & 3
        spun = []
        for d in range(REACH):
            piece = boxes_ref[(((q0 + d) & 7) * NY + j) * REACH + d].astype(f32)
            spun.append([piece] + [pltpu.roll(piece, 32 * turns, 1) for turns in range(1, 4)])

        def joined(first, s):
            value = spun[first][(0 - s) % 4]
            for dd in range(1, 4):
                value = jnp.where(group == dd, spun[first + dd][(dd - s) % 4], value)
            return value

        for s in range(4):
            slot = home * 4 + s
            top = ((code_ref[z, slot] & 4095) - rows_of(z, q0)) & 255
            shift = (table_ref[home, 0, 2 * s] - top) & 255
            low = jnp.where(lane >= top, joined(0, s), spun[8][(0 - s) % 4])
            held[slot] = pltpu.roll(jnp.concatenate([low, joined(4, s)], axis=1), shift, 1)

    loop(32, one_home)

    kinds = lax.broadcasted_iota(jnp.int32, (64, 128), 0)
    chosen = (kinds == (labels_ref[pl.ds(z, 1), :] >> 24)).astype(bf16)
    columns = [mm(chosen, held[:, c, :].astype(bf16)) for c in range(8)]
    loads[0].wait()
    main = full_product(one_ref, jnp.concatenate([column[:48] for column in columns], axis=0), mmt)
    rest = full_product(one_ref, jnp.concatenate([column[48:50] for column in columns], axis=0), mmt)
    rest = jnp.concatenate([rest[64 * k : 64 * k + 64] for k in range(NQ)], axis=1)
    for k in range(NQ):
        for t in range(3):
            to_z[3 * k + t] = main[64 * k : 64 * k + 64, 128 * t : 128 * t + 128].reshape(NZ, 4, 128).astype(bf16)
    to_z[24] = rest.reshape(NZ, 4, 128).astype(bf16)
    pl.semaphore_wait(barrier, 15 + 31)

    def send_z(k):
        other = lax.rem(z + k, NZ)
        remote(to_z.at[:, other], landed.at[:, z], send.at[0], recv.at[0], other * NQ + q, y).start()

    def send_q(k):
        other = lax.rem(q + k, NQ)
        remote(freq_ref.at[:, :, other], freq.at[:, q], send.at[2], recv.at[2], z * NQ + other, y).start()

    loop(NQ, send_q, 1)
    loop(NZ, send_z, 1)
    own = [
        pltpu.make_async_copy(to_z.at[:, z], landed.at[:, z], local.at[0]),
        pltpu.make_async_copy(freq_ref.at[:, :, q], freq.at[:, q], local.at[1]),
    ]
    for copy in own:
        copy.start()

    cos_y, sin_y = quarter_ref[y, 0][None, :], quarter_ref[y, 1][None, :]
    cos = twist_ref[0] * cos_y - twist_ref[1] * sin_y
    sin = twist_ref[1] * cos_y + twist_ref[0] * sin_y

    counts = jnp.zeros((64, 128), f32)
    for k in range(NZ):
        counts = counts + (kinds == (labels_ref[k : k + 1, :] >> 24)).astype(f32)
    inverse = 1.0 / (BOX * jnp.maximum(jnp.sum(counts, axis=1, keepdims=True), 1.0))

    for load in loads[1:]:
        load.wait()
    own[1].wait()
    wait_for(freq.at[:, pl.ds(0, NQ - 1)], send.at[2])
    wait_for(freq.at[:, pl.ds(0, NQ - 1)], recv.at[2])
    col_cos, col_sin = col_twist_ref[0], col_twist_ref[1]
    for h in range(2):
        section = exact_product(col_one_ref, freq[h].reshape(256, 128), mm)
        real = section[:128] * col_cos + section[128:] * col_sin
        imag = section[128:] * col_cos - section[:128] * col_sin
        result = full_product(col_two_ref, jnp.concatenate([real, imag], axis=1), mmt)
        power = (result[:128] * result[:128] + result[128:] * result[128:]) * (1.0 / (NPIX * NPIX))
        for tau in range(32):
            power_ref[0, 4 * h : 4 * h + 4, 128 * tau : 128 * tau + 128] = power[4 * tau : 4 * tau + 4]

    own[0].wait()
    wait_for(landed.at[:, pl.ds(0, 15)], send.at[0])
    wait_for(landed.at[:, pl.ds(0, 15)], recv.at[0])
    last = jnp.sum(landed[24].astype(f32), axis=0)
    for k in range(NQ):
        for t in range(3):
            sums[k, t] = jnp.sum(landed[3 * k + t].astype(f32), axis=0)
        sums[k, 3] = last

    def send_plane(k):
        other = lax.rem(p + k, 32)
        there = other // NY
        remote(sums.at[there], got.at[p], send.at[1], recv.at[1], z * NQ + there, lax.rem(other, NY)).start()

    loop(32, send_plane, 1)
    mine = pltpu.make_async_copy(sums.at[q], got.at[p], local.at[2])
    mine.start()
    mine.wait()
    wait_for(got.at[pl.ds(0, 31)], send.at[1])
    wait_for(got.at[pl.ds(0, 31)], recv.at[1])

    pieces = []
    for a in range(2):
        for t in range(4):
            pieces.append(jnp.concatenate([got[:, t, a, :], got[:, t, 2 + a, :]], axis=0))
    section = full_product(two_ref, jnp.concatenate(pieces, axis=1), mm)
    lanes = lax.broadcasted_iota(jnp.int32, (48, 384), 1)
    pick = (lax.rem(lanes, 48) == lax.broadcasted_iota(jnp.int32, (48, 384), 0)).astype(bf16)
    lanes = lax.broadcasted_iota(jnp.int32, (16, 128), 1)
    pick_rest = (((lanes >> 4) == q) & ((lanes & 1) == lax.broadcasted_iota(jnp.int32, (16, 128), 0))).astype(bf16)
    for a in range(2):
        real = jnp.concatenate([section[:32, 512 * a : 512 * a + 512]] * 2, axis=0)
        imag = jnp.concatenate([section[32:, 512 * a : 512 * a + 512]] * 2, axis=0)
        for part, value in enumerate((real * cos + imag * sin, imag * cos - real * sin)):
            high, low = halves(value)
            total = mmt(pick, high[:, :384]) + mmt(pick, low[:, :384])
            means_ref[0:48, part, a, :] = total * inverse[:48]
            total = mmt(pick_rest, high[:, 384:]) + mmt(pick_rest, low[:, 384:])
            means_ref[48:50, part, a, :] = total[:2] * inverse[48:50]


def rows_of(z, q0):
    return (z * NQ + q0) * 32


def whole_pieces(ref, count):
    return ref.at[pl.ds(0, count)]


def call(kernel, outs, ins, out_specs, scratch=(), collective=None, name=None):
    params = dict(has_side_effects=True, collective_id=collective) if collective is not None else {}
    return pl.pallas_call(
        kernel,
        out_shape=outs,
        in_specs=ins,
        out_specs=out_specs,
        scratch_shapes=list(scratch),
        compiler_params=pltpu.CompilerParams(**params),
        name=name,
    )


def shape(*dims, dtype=bf16):
    return jax.ShapeDtypeStruct(dims, dtype)


def sems(count):
    return pltpu.SemaphoreType.DMA((count,))


def per_device(micrograph, box_tops, box_live, box_class, box_shift):
    consts = {name: jnp.asarray(value) for name, value in tables().items()}
    labels = jnp.where(box_live == 1, box_class, CLASSES)
    codes = ((labels * 4096 + box_tops[..., 1]) * 4096 + box_tops[..., 0]).reshape(NZ, 128)

    shifts = jnp.pad(box_shift.reshape(1, 8), ((0, 0), (0, 120)))
    band, table = call(
        gather_kernel,
        (shape(16, 32, 256), shape(32 + NQ, 1, 128, dtype=jnp.int32)),
        [ANY, VMEM],
        (VMEM, VMEM),
        (sems(5), sems(2), sems(2)),
        collective=0,
        name="gather",
    )(micrograph, shifts)

    freq, boxes = call(
        spread_kernel,
        (shape(2, NZ, 16, 128), shape(32 * REACH, 8, 128)),
        [SMEM, SMEM, VMEM, VMEM, ANY, ANY],
        (VMEM, VMEM),
        (
            pltpu.VMEM((2, 512, 256), bf16),
            pltpu.VMEM((2, 256, 1024), bf16),
            pltpu.VMEM((128, 256), f32),
            pltpu.VMEM((32, REACH, 8, 128), bf16),
            pltpu.VMEM((2, 256, 128), bf16),
            sems(4),
            sems(3),
            sems(3),
        ),
        collective=1,
        name="spread",
    )(codes, table, band, consts["row_twist"], consts["row_one"], consts["row_two"])

    power, means = call(
        sum_kernel,
        (shape(1, 8, NPIX, dtype=f32), shape(CLASSES, 2, 2, 64, dtype=f32)),
        [SMEM, SMEM, VMEM, VMEM, VMEM, ANY, VMEM, VMEM, VMEM, ANY, VMEM, ANY],
        (VMEM, VMEM),
        (
            pltpu.VMEM((2, 512, 256), bf16),
            pltpu.VMEM((2, 256, 256), bf16),
            pltpu.VMEM((2, 256, 256), bf16),
            pltpu.VMEM((128, 8, 256), f32),
            pltpu.VMEM((25, NZ, 4, 128), bf16),
            pltpu.VMEM((25, NZ, 4, 128), bf16),
            pltpu.VMEM((NQ, 4, 4, 128), f32),
            pltpu.VMEM((32, 4, 4, 128), f32),
            pltpu.VMEM((2, NQ, NZ, 2, 128), bf16),
            sems(7),
            sems(3),
            sems(3),
        ),
        collective=2,
        name="sums",
    )(
        codes, table, codes, boxes, freq.reshape(2, NZ, NQ, 2, 128), consts["box_one"], consts["box_two"], consts["box_twist"],
        consts["box_quarter"], consts["col_one"], consts["col_twist"], consts["col_two"],
    )
    return power, means


def solution(mesh):
    in_specs = (P("rows", "half"), P(), P(), P(), P("rows", "half", None, None))
    out_specs = (P("half", "rows", None), P(None, None, "rows", "half"))
    return jax.shard_map(per_device, mesh=mesh, in_specs=in_specs, out_specs=out_specs, check_vma=False)
```

```python
import functools

import jax
import jax.numpy as jnp
import numpy as np
from jax import lax
from jax.experimental import pallas as pl
from jax.experimental.pallas import tpu as pltpu
from jax.sharding import PartitionSpec as P

BOX = 256
CLASSES = 50
NPIX = 4096
NZ, NQ, NY = 16, 8, 4
NBAND = 128
REACH = 9
MESH = pl.DeviceIdType.MESH
f32 = jnp.float32
bf16 = jnp.bfloat16
VMEM = pl.BlockSpec(memory_space=pltpu.VMEM)
SMEM = pl.BlockSpec(memory_space=pltpu.SMEM)
ANY = pl.BlockSpec(memory_space=pl.ANY)


def two_parts(matrix):
    high = matrix.astype(bf16)
    return np.stack([high, (matrix - high.astype(np.float64)).astype(bf16)])


def turn(left, right, length):
    angle = 2.0 * np.pi / length * np.mod(np.multiply.outer(left, right), length)
    return np.cos(angle), np.sin(angle)


@functools.lru_cache(None)
def tables():
    out = {}
    c, s = turn(np.arange(8), np.arange(8), 8)
    eye = np.eye(32)
    out["row_one"] = two_parts(np.concatenate([np.kron(c, eye), np.kron(-s, eye)]))
    angle = np.arange(8)[None] + 1024 * np.arange(4)[:, None]
    c, s = turn(angle, np.arange(512), NPIX)
    out["row_twist"] = np.stack([c, s], axis=1).astype(np.float32)
    c, s = turn(np.arange(128), np.arange(512), 512)
    real = np.concatenate([c, s], axis=1)
    imag = np.concatenate([-s, c], axis=1)
    both = np.stack([real, imag], axis=1).reshape(NZ, NQ, 2, 1024).transpose(1, 0, 2, 3)
    out["row_two"] = two_parts(both.reshape(256, 1024))
    c, s = turn(np.arange(128), np.arange(128), 128)
    real = np.stack([c, s], axis=2)
    imag = np.stack([-s, c], axis=2)
    both = np.concatenate([real, imag]).reshape(256, NZ, NQ, 2).transpose(0, 2, 1, 3)
    out["col_one"] = two_parts(both.reshape(256, 256))
    c, s = turn(np.arange(128), np.arange(32), NPIX)
    out["col_twist"] = np.stack([np.tile(c, (1, 4)), np.tile(s, (1, 4))]).astype(np.float32)
    c, s = turn(np.arange(32), np.arange(32), 32)
    same = np.eye(4)

    def spread(matrix):
        return np.einsum("tm,kl->tklm", matrix, same).reshape(128, 128)

    out["col_two"] = two_parts(np.block([[spread(c), spread(s)], [spread(-s), spread(c)]]))
    c, s = turn(np.arange(256), np.arange(256), 256)
    both = np.stack([c, -s]).reshape(2, NZ, NQ, 2, 256).transpose(2, 1, 0, 3, 4)
    out["box_one"] = two_parts(both.reshape(512, 256))
    c, s = turn(np.arange(32), np.arange(32), 32)
    out["box_two"] = two_parts(np.block([[c, s], [-s, c]]))
    lanes = np.concatenate([np.arange(384) // 48, (np.arange(128) >> 1) & 7])
    c, s = turn(np.arange(64), lanes, 256)
    out["box_twist"] = np.stack([c, s]).astype(np.float32)
    c, s = turn(np.arange(4), lanes, 4)
    out["box_quarter"] = np.stack([c, s], axis=1).reshape(4, 2, 512).astype(np.float32)
    return out


def halves(value):
    high = value.astype(bf16)
    return high, (value - high.astype(f32)).astype(bf16)


def mm(left, right):
    return lax.dot_general(left, right, (((1,), (0,)), ((), ())), preferred_element_type=f32)


def mmt(left, right):
    return lax.dot_general(left, right, (((1,), (1,)), ((), ())), preferred_element_type=f32)


def exact_product(table_ref, value, dot):
    return dot(table_ref[0], value) + dot(table_ref[1], value)


def full_product(table_ref, value, dot):
    high, low = halves(value)
    return dot(table_ref[0], high) + (dot(table_ref[1], high) + dot(table_ref[0], low))


def place():
    rows = lax.axis_index("rows")
    half = lax.axis_index("half")
    z = rows // NQ
    q = rows - z * NQ
    return rows, half, z, q, q * NY + half


def signal(barrier, rows, half):
    pl.semaphore_signal(barrier, inc=1, device_id=(rows, half), device_id_type=MESH)


def remote(src, dst, send, recv, rows, half):
    return pltpu.make_async_remote_copy(
        src_ref=src, dst_ref=dst, send_sem=send, recv_sem=recv, device_id=(rows, half), device_id_type=MESH
    )


def wait_for(ref, sem):
    pltpu.make_async_copy(ref, ref, sem).wait()


def loop(count, body, start=0):
    def step(index, carry):
        body(index)
        return carry

    lax.fori_loop(start, count, step, 0)


def signal_plane(barrier, z, p):
    def greet(k):
        other = lax.rem(p + k, 32)
        signal(barrier, z * NQ + other // NY, lax.rem(other, NY))

    loop(32, greet, 1)


def gather_kernel(mic_ref, shift_ref, band_ref, table_ref, local, send, recv):
    rows, y, z, q, p = place()
    before, after = lax.rem(z + NZ - 1, NZ), lax.rem(z + 1, NZ)
    own = []
    for a in range(4):
        own.append(pltpu.make_async_copy(mic_ref.at[:, pl.ds(256 * a, 256)], band_ref.at[NY * y + a], local.at[a]))
    own.append(pltpu.make_async_copy(shift_ref, table_ref.at[p], local.at[4]))
    for copy in own:
        copy.start()
    barrier = pltpu.get_barrier_semaphore()
    signal_plane(barrier, z, p)
    for k in range(NQ):
        signal(barrier, before * NQ + k, y)
    for copy in own:
        copy.wait()
    pl.semaphore_wait(barrier, 31 + NQ)

    mine = band_ref.at[pl.ds(NY * y, 4)]
    for k in range(1, NY):
        remote(mine, mine, send.at[0], recv.at[0], rows, lax.rem(y + k, NY)).start()
    for k in range(NQ):
        remote(table_ref.at[p], table_ref.at[32 + q], send.at[1], recv.at[1], after * NQ + k, y).start()

    def tell(k):
        other = lax.rem(p + k, 32)
        remote(
            table_ref.at[p], table_ref.at[p], send.at[1], recv.at[1], z * NQ + other // NY, lax.rem(other, NY)
        ).start()

    loop(32, tell, 1)
    wait_for(band_ref.at[pl.ds(0, 12)], send.at[0])
    wait_for(table_ref.at[pl.ds(0, 31 + NQ)], send.at[1])
    wait_for(band_ref.at[pl.ds(0, 12)], recv.at[0])
    wait_for(table_ref.at[pl.ds(0, 31 + NQ)], recv.at[1])


def far_first(count):
    return sorted(range(1, count), key=lambda k: -min(k, count - k))


def main_kernel(
    tops_ref, table_ref, class_ref, live_ref, band_ref, row_twist_ref, box_twist_ref, quarter_ref, col_twist_ref, box_two_ref,
    row_one_hbm, row_two_hbm, box_one_hbm, col_one_hbm, col_two_hbm, power_ref, means_ref,
    row_one_ref, row_two_ref, box_one_ref, col_one_ref, col_two_ref,
    strip, boxes, boxes_in, freq, freq_mid, freq_ready, freq_in, held, to_z, landed, sums, got, local, load_sem, send, recv,
):
    rows, y, z, q, p = place()
    before, after = lax.rem(z + NZ - 1, NZ), lax.rem(z + 1, NZ)
    barrier = pltpu.get_barrier_semaphore()
    loads = []
    for index, (source, target) in enumerate(
        (
            (row_one_hbm, row_one_ref),
            (row_two_hbm, row_two_ref),
            (box_one_hbm, box_one_ref),
            (col_one_hbm, col_one_ref),
            (col_two_hbm, col_two_ref),
        )
    ):
        loads.append(pltpu.make_async_copy(source, target, load_sem.at[index]))
        loads[-1].start()

    for k in far_first(NZ):
        signal(barrier, lax.rem(z + k, NZ) * NQ + q, y)
    loop(32, lambda k: signal(barrier, after * NQ + k // NY, lax.rem(k, NY)))
    signal_plane(barrier, z, p)

    lane = lax.broadcasted_iota(jnp.int32, (32, 256), 1)

    def one_band(d):
        near = q - d
        entry = jnp.where(near >= 0, near * NY + y, 32 + near + NQ)
        home = lax.rem(rows - d + NBAND, NBAND)
        for s in range(4):
            left = tops_ref[(y * 4 + s) * 2 + 1, home] & 4095
            block = left >> 8
            offset = left & 255
            first = band_ref[block].astype(f32)
            second = band_ref[jnp.minimum(block + 1, 15)].astype(f32)
            picked = jnp.where(lane >= offset, first, second)
            shift = (table_ref[entry, 1, s] - offset) & 255
            strip[pl.ds(32 * s, 32), :] = pltpu.roll(picked, shift, 1)
        boxes[:, d] = strip[...].T.reshape(32, 8, 128).astype(bf16)

    loop(REACH, one_band)
    pl.semaphore_wait(barrier, 15 + 63)

    here = p * REACH
    for level in range(NQ):

        @pl.when(q == level)
        def _():
            near, far = level + 1, REACH - 1 - level

            def send_far(k):
                other = lax.rem(p + 16 + k, 32)
                remote(
                    boxes.at[other, pl.ds(near, far)], boxes_in.at[pl.ds(here + near, far)],
                    send.at[2], recv.at[2], before * NQ + other // NY, lax.rem(other, NY),
                ).start()

            def send_near(k):
                other = lax.rem(p + k, 32)
                remote(
                    boxes.at[other, pl.ds(0, near)], boxes_in.at[pl.ds(here, near)],
                    send.at[1], recv.at[1], z * NQ + other // NY, lax.rem(other, NY),
                ).start()

            loop(32, send_far)
            loop(32, send_near, 1)
            pltpu.make_async_copy(boxes.at[p, pl.ds(0, near)], boxes_in.at[pl.ds(here, near)], local.at[0]).start()

    loads[0].wait()
    loads[1].wait()
    real, imag = [], []
    cos_all, sin_all = row_twist_ref[y, 0], row_twist_ref[y, 1]
    for side in range(2):
        pixels = band_ref[:, :].reshape(8, 2, 32, 256)[:, side].reshape(256, 256)
        section = exact_product(row_one_ref, pixels, mm)
        cos = jnp.broadcast_to(cos_all[:, 256 * side : 256 * side + 256][:, None, :], (8, 32, 256)).reshape(256, 256)
        sin = jnp.broadcast_to(sin_all[:, 256 * side : 256 * side + 256][:, None, :], (8, 32, 256)).reshape(256, 256)
        real.append(section[:256] * cos + section[256:] * sin)
        imag.append(section[256:] * cos - section[:256] * sin)
    turned = jnp.concatenate(real + imag, axis=1)
    result = full_product(row_two_ref, turned, mmt).astype(bf16)
    freq[0] = result[:, :128]
    freq[1] = result[:, 128:]

    for k in far_first(NQ):
        other = lax.rem(q + k, NQ)
        remote(freq.at[:, pl.ds(32 * other, 32)], freq_mid.at[:, q], send.at[3], recv.at[3], z * NQ + other, y).start()
    own_mid = pltpu.make_async_copy(freq.at[:, pl.ds(32 * q, 32)], freq_mid.at[:, q], local.at[1])
    own_mid.start()
    own_mid.wait()
    wait_for(freq_mid.at[:, pl.ds(0, NQ - 1)], send.at[3])
    wait_for(freq_mid.at[:, pl.ds(0, NQ - 1)], recv.at[3])
    for h in range(2):
        freq_ready[h] = freq_mid[h].reshape(NQ, NZ, 2, 128)
    for k in far_first(NZ):
        other = lax.rem(z + k, NZ)
        remote(freq_ready.at[:, :, other], freq_in.at[:, :, z], send.at[4], recv.at[4], other * NQ + q, y).start()
    own_freq = pltpu.make_async_copy(freq_ready.at[:, :, z], freq_in.at[:, :, z], local.at[1])
    own_freq.start()

    for level in range(NQ):

        @pl.when(q == level)
        def _():
            near, far = level + 1, REACH - 1 - level
            wait_for(boxes.at[0, pl.ds(0, near)], local.at[0])
            wait_for(boxes.at[pl.ds(0, 32), pl.ds(0, far)], send.at[2])
            wait_for(boxes.at[pl.ds(0, 31), pl.ds(0, near)], send.at[1])
            wait_for(boxes_in.at[pl.ds(0, 144 - near)], recv.at[1])

    wait_for(boxes_in.at[pl.ds(0, 144)], recv.at[2])

    lane = lax.broadcasted_iota(jnp.int32, (8, 128), 1)
    group = lane >> 5

    def one_home(home):
        q0 = home >> 2
        j = home & 3
        spun = []
        for d in range(REACH):
            piece = boxes_in[(((q0 + d) & 7) * NY + j) * REACH + d].astype(f32)
            spun.append([piece] + [pltpu.roll(piece, 32 * turns, 1) for turns in range(1, 4)])

        def joined(first, s):
            value = spun[first][(0 - s) % 4]
            for dd in range(1, 4):
                value = jnp.where(group == dd, spun[first + dd][(dd - s) % 4], value)
            return value

        for s in range(4):
            slot = home * 4 + s
            band = z * NQ + q0
            top = (tops_ref[(j * 4 + s) * 2, band] - band * 32) & 255
            shift = (table_ref[home, 0, s] - top) & 255
            low = jnp.where(lane >= top, joined(0, s), spun[8][(0 - s) % 4])
            held[slot] = pltpu.roll(jnp.concatenate([low, joined(4, s)], axis=1), shift, 1)

    loop(32, one_home)

    labels = jnp.where(live_ref[...] == 1, class_ref[...], CLASSES)
    plane_labels = pltpu.roll(labels, lax.rem(NBAND - z * NQ, NBAND), 1)
    kind_lane = lax.broadcasted_iota(jnp.int32, (16, 128), 1)
    chosen = jnp.concatenate([(plane_labels[:, k : k + 1] == kind_lane).astype(f32) for k in range(NQ)], axis=0)
    chosen = chosen.T[:64].astype(bf16)
    columns = [mm(chosen, held[:, c, :].astype(bf16)) for c in range(8)]
    loads[2].wait()
    main = full_product(box_one_ref, jnp.concatenate([column[:48] for column in columns], axis=0), mmt)
    rest = full_product(box_one_ref, jnp.concatenate([column[48:50] for column in columns], axis=0), mmt)
    rest = jnp.concatenate([rest[64 * k : 64 * k + 64] for k in range(NQ)], axis=1)
    for k in range(NQ):
        for t in range(3):
            to_z[3 * k + t] = main[64 * k : 64 * k + 64, 128 * t : 128 * t + 128].reshape(NZ, 4, 128).astype(bf16)
    to_z[24] = rest.reshape(NZ, 4, 128).astype(bf16)

    for k in far_first(NZ):
        other = lax.rem(z + k, NZ)
        remote(to_z.at[:, other], landed.at[:, z], send.at[0], recv.at[0], other * NQ + q, y).start()
    own = pltpu.make_async_copy(to_z.at[:, z], landed.at[:, z], local.at[2])
    own.start()

    cos_y, sin_y = quarter_ref[y, 0][None, :], quarter_ref[y, 1][None, :]
    cos = box_twist_ref[0] * cos_y - box_twist_ref[1] * sin_y
    sin = box_twist_ref[1] * cos_y + box_twist_ref[0] * sin_y

    kinds = lax.broadcasted_iota(jnp.int32, (64, 128), 0)
    counts = jnp.zeros((64, 128), f32)
    for k in range(16):
        counts = counts + (kinds == labels[k : k + 1, :]).astype(f32)
    inverse = 1.0 / (BOX * jnp.maximum(jnp.sum(counts, axis=1, keepdims=True), 1.0))

    loads[3].wait()
    loads[4].wait()
    own_freq.wait()
    wait_for(freq_in.at[:, :, pl.ds(0, NZ - 1)], send.at[4])
    wait_for(freq_in.at[:, :, pl.ds(0, NZ - 1)], recv.at[4])
    col_cos, col_sin = col_twist_ref[0], col_twist_ref[1]
    for h in range(2):
        section = exact_product(col_one_ref, freq_in[h].reshape(256, 128), mm)
        real = section[:128] * col_cos + section[128:] * col_sin
        imag = section[128:] * col_cos - section[:128] * col_sin
        result = full_product(col_two_ref, jnp.concatenate([real, imag], axis=1), mmt)
        power = (result[:128] * result[:128] + result[128:] * result[128:]) * (1.0 / (NPIX * NPIX))
        for tau in range(32):
            power_ref[0, 4 * h : 4 * h + 4, 128 * tau : 128 * tau + 128] = power[4 * tau : 4 * tau + 4]

    own.wait()
    wait_for(landed.at[:, pl.ds(0, 15)], send.at[0])
    wait_for(landed.at[:, pl.ds(0, 15)], recv.at[0])
    last = jnp.sum(landed[24].astype(f32), axis=0)
    for k in range(NQ):
        for t in range(3):
            sums[k, t] = jnp.sum(landed[3 * k + t].astype(f32), axis=0)
        sums[k, 3] = last

    def send_plane(k):
        other = lax.rem(p + k, 32)
        there = other // NY
        remote(sums.at[there], got.at[p], send.at[5], recv.at[5], z * NQ + there, lax.rem(other, NY)).start()

    loop(32, send_plane, 1)
    mine = pltpu.make_async_copy(sums.at[q], got.at[p], local.at[3])
    mine.start()
    mine.wait()
    wait_for(got.at[pl.ds(0, 31)], send.at[5])
    wait_for(got.at[pl.ds(0, 31)], recv.at[5])

    pieces = []
    for a in range(2):
        for t in range(4):
            pieces.append(jnp.concatenate([got[:, t, a, :], got[:, t, 2 + a, :]], axis=0))
    section = full_product(box_two_ref, jnp.concatenate(pieces, axis=1), mm)
    lanes = lax.broadcasted_iota(jnp.int32, (48, 384), 1)
    pick = (lax.rem(lanes, 48) == lax.broadcasted_iota(jnp.int32, (48, 384), 0)).astype(bf16)
    lanes = lax.broadcasted_iota(jnp.int32, (16, 128), 1)
    pick_rest = (((lanes >> 4) == q) & ((lanes & 1) == lax.broadcasted_iota(jnp.int32, (16, 128), 0))).astype(bf16)
    for a in range(2):
        real = jnp.concatenate([section[:32, 512 * a : 512 * a + 512]] * 2, axis=0)
        imag = jnp.concatenate([section[32:, 512 * a : 512 * a + 512]] * 2, axis=0)
        for part, value in enumerate((real * cos + imag * sin, imag * cos - real * sin)):
            high, low = halves(value)
            total = mmt(pick, high[:, :384]) + mmt(pick, low[:, :384])
            means_ref[0:48, part, a, :] = total * inverse[:48]
            total = mmt(pick_rest, high[:, 384:]) + mmt(pick_rest, low[:, 384:])
            means_ref[48:50, part, a, :] = total[:2] * inverse[48:50]


def call(kernel, outs, ins, out_specs, scratch=(), collective=None, name=None):
    params = dict(has_side_effects=True, collective_id=collective) if collective is not None else {}
    return pl.pallas_call(
        kernel,
        out_shape=outs,
        in_specs=ins,
        out_specs=out_specs,
        scratch_shapes=list(scratch),
        compiler_params=pltpu.CompilerParams(**params),
        name=name,
    )


def shape(*dims, dtype=bf16):
    return jax.ShapeDtypeStruct(dims, dtype)


def sems(count):
    return pltpu.SemaphoreType.DMA((count,))


def per_device(micrograph, box_tops, box_live, box_class, box_shift):
    consts = {name: jnp.asarray(value) for name, value in tables().items()}
    tops = box_tops.transpose(1, 2, 3, 0).reshape(32, NBAND)
    classes = box_class.transpose(1, 2, 0).reshape(16, NBAND)
    live = box_live.transpose(1, 2, 0).reshape(16, NBAND)
    shifts = box_shift.transpose(0, 1, 3, 2).reshape(2, 4)

    band, table = call(
        gather_kernel,
        (shape(16, 32, 256), shape(32 + NQ, 2, 4, dtype=jnp.int32)),
        [ANY, VMEM],
        (VMEM, VMEM),
        (sems(5), sems(2), sems(2)),
        collective=0,
        name="gather",
    )(micrograph, shifts)

    return call(
        main_kernel,
        (shape(1, 8, NPIX, dtype=f32), shape(CLASSES, 2, 2, 64, dtype=f32)),
        [SMEM, SMEM] + [VMEM] * 8 + [ANY] * 5,
        (VMEM, VMEM),
        (
            pltpu.VMEM((2, 512, 256), bf16),
            pltpu.VMEM((2, 256, 1024), bf16),
            pltpu.VMEM((2, 512, 256), bf16),
            pltpu.VMEM((2, 256, 256), bf16),
            pltpu.VMEM((2, 256, 256), bf16),
            pltpu.VMEM((128, 256), f32),
            pltpu.VMEM((32, REACH, 8, 128), bf16),
            pltpu.VMEM((32 * REACH, 8, 128), bf16),
            pltpu.VMEM((2, 256, 128), bf16),
            pltpu.VMEM((2, NQ, 32, 128), bf16),
            pltpu.VMEM((2, NQ, NZ, 2, 128), bf16),
            pltpu.VMEM((2, NQ, NZ, 2, 128), bf16),
            pltpu.VMEM((128, 8, 256), f32),
            pltpu.VMEM((25, NZ, 4, 128), bf16),
            pltpu.VMEM((25, NZ, 4, 128), bf16),
            pltpu.VMEM((NQ, 4, 4, 128), f32),
            pltpu.VMEM((32, 4, 4, 128), f32),
            sems(4),
            sems(5),
            sems(6),
            sems(6),
        ),
        collective=1,
        name="main",
    )(
        tops, table, classes, live, band, consts["row_twist"], consts["box_twist"], consts["box_quarter"], consts["col_twist"],
        consts["box_two"], consts["row_one"], consts["row_two"], consts["box_one"], consts["col_one"], consts["col_two"],
    )


def solution(mesh):
    in_specs = (P("rows", "half"), P(), P(), P(), P("rows", "half", None, None))
    out_specs = (P("half", "rows", None), P(None, None, "rows", "half"))
    return jax.shard_map(per_device, mesh=mesh, in_specs=in_specs, out_specs=out_specs, check_vma=False)
```

```python
import functools

import jax
import jax.numpy as jnp
import numpy as np
from jax import lax
from jax.experimental import pallas as pl
from jax.experimental.pallas import tpu as pltpu
from jax.sharding import PartitionSpec as P

BOX = 256
CLASSES = 50
NPIX = 4096
NZ, NQ, NY = 16, 8, 4
NBAND = 128
REACH = 9
MESH = pl.DeviceIdType.MESH
f32 = jnp.float32
bf16 = jnp.bfloat16
VMEM = pl.BlockSpec(memory_space=pltpu.VMEM)
SMEM = pl.BlockSpec(memory_space=pltpu.SMEM)
ANY = pl.BlockSpec(memory_space=pl.ANY)


def two_parts(matrix):
    high = matrix.astype(bf16)
    return np.stack([high, (matrix - high.astype(np.float64)).astype(bf16)])


def turn(left, right, length):
    angle = 2.0 * np.pi / length * np.mod(np.multiply.outer(left, right), length)
    return np.cos(angle), np.sin(angle)


@functools.lru_cache(None)
def tables():
    out = {}
    c, s = turn(np.arange(8), np.arange(8), 8)
    eye = np.eye(32)
    out["row_one"] = two_parts(np.concatenate([np.kron(c, eye), np.kron(-s, eye)]))
    angle = np.arange(8)[None] + 1024 * np.arange(4)[:, None]
    c, s = turn(angle, np.arange(512), NPIX)
    out["row_twist"] = np.stack([c, s], axis=1).astype(np.float32)
    c, s = turn(np.arange(128), np.arange(512), 512)
    real = np.concatenate([c, s], axis=1)
    imag = np.concatenate([-s, c], axis=1)
    both = np.stack([real, imag], axis=1).reshape(NZ, NQ, 2, 1024).transpose(1, 0, 2, 3)
    out["row_two"] = two_parts(both.reshape(256, 1024))
    c, s = turn(np.arange(128), np.arange(128), 128)
    real = np.stack([c, s], axis=2)
    imag = np.stack([-s, c], axis=2)
    both = np.concatenate([real, imag]).reshape(256, NZ, NQ, 2).transpose(0, 2, 1, 3)
    out["col_one"] = two_parts(both.reshape(256, 256))
    c, s = turn(np.arange(128), np.arange(32), NPIX)
    out["col_twist"] = np.stack([np.tile(c, (1, 4)), np.tile(s, (1, 4))]).astype(np.float32)
    c, s = turn(np.arange(32), np.arange(32), 32)
    same = np.eye(4)

    def spread(matrix):
        return np.einsum("tm,kl->tklm", matrix, same).reshape(128, 128)

    out["col_two"] = two_parts(np.block([[spread(c), spread(s)], [spread(-s), spread(c)]]))
    c, s = turn(np.arange(256), np.arange(256), 256)
    both = np.stack([c, -s]).reshape(2, NZ, NQ, 2, 256).transpose(2, 1, 0, 3, 4)
    out["box_one"] = two_parts(both.reshape(512, 256))
    c, s = turn(np.arange(32), np.arange(32), 32)
    out["box_two"] = two_parts(np.block([[c, s], [-s, c]]))
    lanes = np.concatenate([np.arange(384) // 48, (np.arange(128) >> 1) & 7])
    c, s = turn(np.arange(64), lanes, 256)
    out["box_twist"] = np.stack([c, s]).astype(np.float32)
    c, s = turn(np.arange(4), lanes, 4)
    out["box_quarter"] = np.stack([c, s], axis=1).reshape(4, 2, 512).astype(np.float32)
    return out


def halves(value):
    high = value.astype(bf16)
    return high, (value - high.astype(f32)).astype(bf16)


def mm(left, right):
    return lax.dot_general(left, right, (((1,), (0,)), ((), ())), preferred_element_type=f32)


def mmt(left, right):
    return lax.dot_general(left, right, (((1,), (1,)), ((), ())), preferred_element_type=f32)


def exact_product(table_ref, value, dot):
    return dot(table_ref[0], value) + dot(table_ref[1], value)


def full_product(table_ref, value, dot):
    high, low = halves(value)
    return dot(table_ref[0], high) + (dot(table_ref[1], high) + dot(table_ref[0], low))


def place():
    rows = lax.axis_index("rows")
    half = lax.axis_index("half")
    z = rows // NQ
    q = rows - z * NQ
    return rows, half, z, q, q * NY + half


def signal(barrier, rows, half):
    pl.semaphore_signal(barrier, inc=1, device_id=(rows, half), device_id_type=MESH)


def remote(src, dst, send, recv, rows, half):
    return pltpu.make_async_remote_copy(
        src_ref=src, dst_ref=dst, send_sem=send, recv_sem=recv, device_id=(rows, half), device_id_type=MESH
    )


def wait_for(ref, sem):
    pltpu.make_async_copy(ref, ref, sem).wait()


def loop(count, body, start=0, unroll=1):
    def step(index, carry):
        body(index)
        return carry

    lax.fori_loop(start, count, step, 0, unroll=unroll)


def signal_plane(barrier, z, p):
    def greet(k):
        other = lax.rem(p + k, 32)
        signal(barrier, z * NQ + other // NY, lax.rem(other, NY))

    loop(32, greet, 1)


def far_first(count):
    return sorted(range(1, count), key=lambda k: -min(k, count - k))


def main_kernel(
    tops_ref, shift_ref, class_ref, live_ref, mic_ref, row_twist_ref, box_twist_ref, quarter_ref, col_twist_ref, box_two_ref,
    row_one_hbm, row_two_hbm, box_one_hbm, col_one_hbm, col_two_hbm, power_ref, means_ref,
    row_one_ref, row_two_ref, box_one_ref, col_one_ref, col_two_ref, band_ref, table_in, table_ref,
    boxes, boxes_in, freq, freq_mid, freq_ready, freq_in, held, to_z, landed, sums, got, local, load_sem, send, recv,
):
    rows, y, z, q, p = place()
    before, after = lax.rem(z + NZ - 1, NZ), lax.rem(z + 1, NZ)
    barrier = pltpu.get_barrier_semaphore()
    for k in far_first(NZ):
        signal(barrier, lax.rem(z + k, NZ) * NQ + q, y)
    loop(32, lambda k: signal(barrier, after * NQ + k // NY, lax.rem(k, NY)))
    loop(NQ, lambda k: signal(barrier, before * NQ + k, y))
    signal_plane(barrier, z, p)

    own = [pltpu.make_async_copy(shift_ref, table_in.at[p], local.at[4])]
    for a in range(4):
        own.append(pltpu.make_async_copy(mic_ref.at[:, pl.ds(256 * a, 256)], band_ref.at[NY * y + a], local.at[a]))
    for copy in own:
        copy.start()
    loads = []
    for index, (source, target) in enumerate(
        (
            (row_one_hbm, row_one_ref),
            (row_two_hbm, row_two_ref),
            (box_one_hbm, box_one_ref),
            (col_one_hbm, col_one_ref),
            (col_two_hbm, col_two_ref),
        )
    ):
        loads.append(pltpu.make_async_copy(source, target, load_sem.at[index]))
        loads[-1].start()
    for copy in own:
        copy.wait()
    pl.semaphore_wait(barrier, 15 + 63 + NQ)

    mine = band_ref.at[pl.ds(NY * y, 4)]
    for k in (2, 1, 3):
        remote(mine, mine, send.at[6], recv.at[6], rows, lax.rem(y + k, NY)).start()
    for k in range(NQ):
        remote(table_in.at[p], table_in.at[32 + q], send.at[7], recv.at[7], after * NQ + k, y).start()

    def tell(k):
        other = lax.rem(p + k, 32)
        remote(
            table_in.at[p], table_in.at[p], send.at[7], recv.at[7], z * NQ + other // NY, lax.rem(other, NY)
        ).start()

    loop(32, tell, 1)
    wait_for(table_in.at[pl.ds(0, 31 + NQ)], recv.at[7])
    to_scalar = pltpu.make_async_copy(table_in, table_ref, local.at[0])
    to_scalar.start()
    wait_for(band_ref.at[pl.ds(0, 12)], recv.at[6])
    to_scalar.wait()

    lane = lax.broadcasted_iota(jnp.int32, (32, 256), 1)

    def one_band(d):
        near = q - d
        entry = jnp.where(near >= 0, near * NY + y, 32 + near + NQ)
        home = lax.rem(rows - d + NBAND, NBAND)
        strips = []
        for s in range(4):
            left = tops_ref[(y * 4 + s) * 2 + 1, home] & 4095
            block = left >> 8
            offset = left & 255
            first = band_ref[block].astype(f32)
            second = band_ref[jnp.minimum(block + 1, 15)].astype(f32)
            picked = jnp.where(lane >= offset, first, second)
            shift = (table_ref[entry, 1, s] - offset) & 255
            strips.append(pltpu.roll(picked, shift, 1))
        boxes[:, d] = jnp.concatenate(strips, axis=0).T.reshape(32, 8, 128).astype(bf16)

    loop(REACH, one_band, unroll=3)

    here = p * REACH
    for level in range(NQ):

        @pl.when(q == level)
        def _():
            near, far = level + 1, REACH - 1 - level
            pltpu.make_async_copy(boxes.at[p, pl.ds(0, near)], boxes_in.at[pl.ds(here, near)], local.at[0]).start()
            for e in (0, 1, 3, 2):
                side = lax.rem(y + e, NY)
                group = (NY - e) % NY

                def send_both(k):
                    there = lax.rem(q + k, NQ)
                    target = there * NY + side
                    remote(
                        boxes.at[target, pl.ds(near, far)], boxes_in.at[pl.ds(here + near, far)],
                        send.at[2], recv.at[12 + group], before * NQ + there, side,
                    ).start()
                    remote(
                        boxes.at[target, pl.ds(0, near)], boxes_in.at[pl.ds(here, near)],
                        send.at[1], recv.at[8 + group], z * NQ + there, side,
                    ).start()

                def send_far_only(k):
                    there = lax.rem(q + k, NQ)
                    remote(
                        boxes.at[there * NY + side, pl.ds(near, far)], boxes_in.at[pl.ds(here + near, far)],
                        send.at[2], recv.at[12 + group], before * NQ + there, side,
                    ).start()

                loop(NQ, send_both, 1)
                if e == 0:
                    send_far_only(0)
                else:
                    send_both(0)

    loads[0].wait()
    loads[1].wait()
    real, imag = [], []
    cos_all, sin_all = row_twist_ref[y, 0], row_twist_ref[y, 1]
    for side in range(2):
        pixels = band_ref[:, :].reshape(8, 2, 32, 256)[:, side].reshape(256, 256)
        section = exact_product(row_one_ref, pixels, mm)
        cos = jnp.broadcast_to(cos_all[:, 256 * side : 256 * side + 256][:, None, :], (8, 32, 256)).reshape(256, 256)
        sin = jnp.broadcast_to(sin_all[:, 256 * side : 256 * side + 256][:, None, :], (8, 32, 256)).reshape(256, 256)
        real.append(section[:256] * cos + section[256:] * sin)
        imag.append(section[256:] * cos - section[:256] * sin)
    turned = jnp.concatenate(real + imag, axis=1)
    result = full_product(row_two_ref, turned, mmt).astype(bf16)
    freq[0] = result[:, :128]
    freq[1] = result[:, 128:]

    for k in far_first(NQ):
        other = lax.rem(q + k, NQ)
        remote(freq.at[:, pl.ds(32 * other, 32)], freq_mid.at[:, q], send.at[3], recv.at[3], z * NQ + other, y).start()
    own_mid = pltpu.make_async_copy(freq.at[:, pl.ds(32 * q, 32)], freq_mid.at[:, q], local.at[1])
    own_mid.start()
    own_mid.wait()
    wait_for(freq_mid.at[:, pl.ds(0, NQ - 1)], send.at[3])
    wait_for(freq_mid.at[:, pl.ds(0, NQ - 1)], recv.at[3])
    for h in range(2):
        freq_ready[h] = freq_mid[h].reshape(NQ, NZ, 2, 128)
    for k in far_first(NZ):
        other = lax.rem(z + k, NZ)
        remote(freq_ready.at[:, :, other], freq_in.at[:, :, z], send.at[4], recv.at[4], other * NQ + q, y).start()
    own_freq = pltpu.make_async_copy(freq_ready.at[:, :, z], freq_in.at[:, :, z], local.at[1])
    own_freq.start()

    lane = lax.broadcasted_iota(jnp.int32, (8, 128), 1)
    group = lane >> 5

    def one_home(q0, j):
        home = q0 * NY + j
        spun = []
        for d in range(REACH):
            piece = boxes_in[(((q0 + d) & 7) * NY + j) * REACH + d].astype(f32)
            spun.append([piece] + [pltpu.roll(piece, 32 * turns, 1) for turns in range(1, 4)])

        def joined(first, s):
            value = spun[first][(0 - s) % 4]
            for dd in range(1, 4):
                value = jnp.where(group == dd, spun[first + dd][(dd - s) % 4], value)
            return value

        for s in range(4):
            slot = home * 4 + s
            band = z * NQ + q0
            top = (tops_ref[(j * 4 + s) * 2, band] - band * 32) & 255
            shift = (table_ref[home, 0, s] - top) & 255
            low = jnp.where(lane >= top, joined(0, s), spun[8][(0 - s) % 4])
            held[slot] = pltpu.roll(jnp.concatenate([low, joined(4, s)], axis=1), shift, 1)

    for g in (0, 1, 3, 2):
        if g == 0:
            for level in range(NQ):

                @pl.when(q == level)
                def _():
                    wait_for(boxes_in.at[pl.ds(0, 36 - (level + 1))], recv.at[8])
                    wait_for(boxes_in.at[pl.ds(0, level + 1)], local.at[0])

        else:
            wait_for(boxes_in.at[pl.ds(0, 36)], recv.at[8 + g])
        wait_for(boxes_in.at[pl.ds(0, 36)], recv.at[12 + g])
        j = lax.rem(y + g, NY)
        loop(NQ, lambda q0: one_home(q0, j), unroll=4)

    labels = jnp.where(live_ref[...] == 1, class_ref[...], CLASSES)
    plane_labels = pltpu.roll(labels, lax.rem(NBAND - z * NQ, NBAND), 1)
    kind_lane = lax.broadcasted_iota(jnp.int32, (16, 128), 1)
    chosen = jnp.concatenate([(plane_labels[:, k : k + 1] == kind_lane).astype(f32) for k in range(NQ)], axis=0)
    chosen = chosen.T[:64].astype(bf16)
    columns = [mm(chosen, held[:, c, :].astype(bf16)) for c in range(8)]
    loads[2].wait()
    main = full_product(box_one_ref, jnp.concatenate([column[:48] for column in columns], axis=0), mmt)
    rest = full_product(box_one_ref, jnp.concatenate([column[48:50] for column in columns], axis=0), mmt)
    rest = jnp.concatenate([rest[64 * k : 64 * k + 64] for k in range(NQ)], axis=1)
    for k in range(NQ):
        for t in range(3):
            to_z[3 * k + t] = main[64 * k : 64 * k + 64, 128 * t : 128 * t + 128].reshape(NZ, 4, 128).astype(bf16)
    to_z[24] = rest.reshape(NZ, 4, 128).astype(bf16)

    for k in far_first(NZ):
        other = lax.rem(z + k, NZ)
        remote(to_z.at[:, other], landed.at[:, z], send.at[0], recv.at[0], other * NQ + q, y).start()
    own = pltpu.make_async_copy(to_z.at[:, z], landed.at[:, z], local.at[2])
    own.start()

    cos_y, sin_y = quarter_ref[y, 0][None, :], quarter_ref[y, 1][None, :]
    cos = box_twist_ref[0] * cos_y - box_twist_ref[1] * sin_y
    sin = box_twist_ref[1] * cos_y + box_twist_ref[0] * sin_y

    kinds = lax.broadcasted_iota(jnp.int32, (64, 128), 0)
    counts = jnp.zeros((64, 128), f32)
    for k in range(16):
        counts = counts + (kinds == labels[k : k + 1, :]).astype(f32)
    inverse = 1.0 / (BOX * jnp.maximum(jnp.sum(counts, axis=1, keepdims=True), 1.0))

    loads[3].wait()
    loads[4].wait()
    own_freq.wait()
    wait_for(freq_in.at[:, :, pl.ds(0, NZ - 1)], send.at[4])
    wait_for(freq_in.at[:, :, pl.ds(0, NZ - 1)], recv.at[4])
    col_cos, col_sin = col_twist_ref[0], col_twist_ref[1]
    for h in range(2):
        section = exact_product(col_one_ref, freq_in[h].reshape(256, 128), mm)
        real = section[:128] * col_cos + section[128:] * col_sin
        imag = section[128:] * col_cos - section[:128] * col_sin
        result = full_product(col_two_ref, jnp.concatenate([real, imag], axis=1), mmt)
        power = (result[:128] * result[:128] + result[128:] * result[128:]) * (1.0 / (NPIX * NPIX))
        for tau in range(32):
            power_ref[0, 4 * h : 4 * h + 4, 128 * tau : 128 * tau + 128] = power[4 * tau : 4 * tau + 4]

    own.wait()
    wait_for(landed.at[:, pl.ds(0, 15)], send.at[0])
    wait_for(landed.at[:, pl.ds(0, 15)], recv.at[0])
    last = jnp.sum(landed[24].astype(f32), axis=0)
    for k in range(NQ):
        for t in range(3):
            sums[k, t] = jnp.sum(landed[3 * k + t].astype(f32), axis=0)
        sums[k, 3] = last

    for k in far_first(32):
        other = lax.rem(p + k, 32)
        there = other // NY
        remote(sums.at[there], got.at[p], send.at[5], recv.at[5], z * NQ + there, lax.rem(other, NY)).start()
    mine = pltpu.make_async_copy(sums.at[q], got.at[p], local.at[3])
    mine.start()
    mine.wait()
    for level in range(NQ):

        @pl.when(q == level)
        def _():
            wait_for(boxes.at[pl.ds(0, 32), pl.ds(0, REACH - 1 - level)], send.at[2])
            wait_for(boxes.at[pl.ds(0, 31), pl.ds(0, level + 1)], send.at[1])

    wait_for(band_ref.at[pl.ds(0, 12)], send.at[6])
    wait_for(table_in.at[pl.ds(0, 31 + NQ)], send.at[7])
    wait_for(got.at[pl.ds(0, 31)], send.at[5])
    wait_for(got.at[pl.ds(0, 31)], recv.at[5])

    pieces = []
    for a in range(2):
        for t in range(4):
            pieces.append(jnp.concatenate([got[:, t, a, :], got[:, t, 2 + a, :]], axis=0))
    section = full_product(box_two_ref, jnp.concatenate(pieces, axis=1), mm)
    lanes = lax.broadcasted_iota(jnp.int32, (48, 384), 1)
    pick = (lax.rem(lanes, 48) == lax.broadcasted_iota(jnp.int32, (48, 384), 0)).astype(bf16)
    lanes = lax.broadcasted_iota(jnp.int32, (16, 128), 1)
    pick_rest = (((lanes >> 4) == q) & ((lanes & 1) == lax.broadcasted_iota(jnp.int32, (16, 128), 0))).astype(bf16)
    for a in range(2):
        real = jnp.concatenate([section[:32, 512 * a : 512 * a + 512]] * 2, axis=0)
        imag = jnp.concatenate([section[32:, 512 * a : 512 * a + 512]] * 2, axis=0)
        for part, value in enumerate((real * cos + imag * sin, imag * cos - real * sin)):
            high, low = halves(value)
            total = mmt(pick, high[:, :384]) + mmt(pick, low[:, :384])
            means_ref[0:48, part, a, :] = total * inverse[:48]
            total = mmt(pick_rest, high[:, 384:]) + mmt(pick_rest, low[:, 384:])
            means_ref[48:50, part, a, :] = total[:2] * inverse[48:50]


def call(kernel, outs, ins, out_specs, scratch=(), collective=None, name=None):
    params = dict(has_side_effects=True, collective_id=collective) if collective is not None else {}
    return pl.pallas_call(
        kernel,
        out_shape=outs,
        in_specs=ins,
        out_specs=out_specs,
        scratch_shapes=list(scratch),
        compiler_params=pltpu.CompilerParams(**params),
        name=name,
    )


def shape(*dims, dtype=bf16):
    return jax.ShapeDtypeStruct(dims, dtype)


def sems(count):
    return pltpu.SemaphoreType.DMA((count,))


def per_device(micrograph, box_tops, box_live, box_class, box_shift):
    consts = {name: jnp.asarray(value) for name, value in tables().items()}
    tops = box_tops.transpose(1, 2, 3, 0).reshape(32, NBAND)
    classes = box_class.transpose(1, 2, 0).reshape(16, NBAND)
    live = box_live.transpose(1, 2, 0).reshape(16, NBAND)
    shifts = box_shift.transpose(0, 1, 3, 2).reshape(2, 4)

    return call(
        main_kernel,
        (shape(1, 8, NPIX, dtype=f32), shape(CLASSES, 2, 2, 64, dtype=f32)),
        [SMEM, VMEM, VMEM, VMEM, ANY] + [VMEM] * 5 + [ANY] * 5,
        (VMEM, VMEM),
        (
            pltpu.VMEM((2, 512, 256), bf16),
            pltpu.VMEM((2, 256, 1024), bf16),
            pltpu.VMEM((2, 512, 256), bf16),
            pltpu.VMEM((2, 256, 256), bf16),
            pltpu.VMEM((2, 256, 256), bf16),
            pltpu.VMEM((16, 32, 256), bf16),
            pltpu.VMEM((32 + NQ, 2, 4), jnp.int32),
            pltpu.SMEM((32 + NQ, 2, 4), jnp.int32),
            pltpu.VMEM((32, REACH, 8, 128), bf16),
            pltpu.VMEM((32 * REACH, 8, 128), bf16),
            pltpu.VMEM((2, 256, 128), bf16),
            pltpu.VMEM((2, NQ, 32, 128), bf16),
            pltpu.VMEM((2, NQ, NZ, 2, 128), bf16),
            pltpu.VMEM((2, NQ, NZ, 2, 128), bf16),
            pltpu.VMEM((128, 8, 256), f32),
            pltpu.VMEM((25, NZ, 4, 128), bf16),
            pltpu.VMEM((25, NZ, 4, 128), bf16),
            pltpu.VMEM((NQ, 4, 4, 128), f32),
            pltpu.VMEM((32, 4, 4, 128), f32),
            sems(5),
            sems(5),
            sems(8),
            sems(16),
        ),
        collective=0,
        name="main",
    )(
        tops, shifts, classes, live, micrograph, consts["row_twist"], consts["box_twist"], consts["box_quarter"], consts["col_twist"],
        consts["box_two"], consts["row_one"], consts["row_two"], consts["box_one"], consts["col_one"], consts["col_two"],
    )


def solution(mesh):
    in_specs = (P("rows", "half"), P(), P(), P(), P("rows", "half", None, None))
    out_specs = (P("half", "rows", None), P(None, None, "rows", "half"))
    return jax.shard_map(per_device, mesh=mesh, in_specs=in_specs, out_specs=out_specs, check_vma=False)
```

```python
import functools

import jax
import jax.numpy as jnp
import numpy as np
from jax import lax
from jax.experimental import pallas as pl
from jax.experimental.pallas import tpu as pltpu
from jax.sharding import PartitionSpec as P

BOX = 256
CLASSES = 50
NPIX = 4096
NZ, NQ, NY = 16, 8, 4
NBAND = 128
REACH = 9
MESH = pl.DeviceIdType.MESH
f32 = jnp.float32
bf16 = jnp.bfloat16
VMEM = pl.BlockSpec(memory_space=pltpu.VMEM)
SMEM = pl.BlockSpec(memory_space=pltpu.SMEM)
ANY = pl.BlockSpec(memory_space=pl.ANY)


def two_parts(matrix):
    high = matrix.astype(bf16)
    return np.stack([high, (matrix - high.astype(np.float64)).astype(bf16)])


def turn(left, right, length):
    angle = 2.0 * np.pi / length * np.mod(np.multiply.outer(left, right), length)
    return np.cos(angle), np.sin(angle)


@functools.lru_cache(None)
def tables():
    out = {}
    c, s = turn(np.arange(8), np.arange(8), 8)
    eye = np.eye(32)
    out["row_one"] = two_parts(np.concatenate([np.kron(c, eye), np.kron(-s, eye)]))
    angle = np.arange(8)[None] + 1024 * np.arange(4)[:, None]
    c, s = turn(angle, np.arange(512), NPIX)
    out["row_twist"] = np.stack([c, s], axis=1).astype(np.float32)
    c, s = turn(np.arange(128), np.arange(512), 512)
    real = np.concatenate([c, s], axis=1)
    imag = np.concatenate([-s, c], axis=1)
    both = np.stack([real, imag], axis=1).reshape(NZ, NQ, 2, 1024).transpose(1, 0, 2, 3)
    out["row_two"] = two_parts(both.reshape(256, 1024))
    c, s = turn(np.arange(128), np.arange(128), 128)
    real = np.stack([c, s], axis=2)
    imag = np.stack([-s, c], axis=2)
    both = np.concatenate([real, imag]).reshape(256, NZ, NQ, 2).transpose(0, 2, 1, 3)
    out["col_one"] = two_parts(both.reshape(256, 256))
    c, s = turn(np.arange(128), np.arange(32), NPIX)
    out["col_twist"] = np.stack([np.tile(c, (1, 4)), np.tile(s, (1, 4))]).astype(np.float32)
    c, s = turn(np.arange(32), np.arange(32), 32)
    same = np.eye(4)

    def spread(matrix):
        return np.einsum("tm,kl->tklm", matrix, same).reshape(128, 128)

    out["col_two"] = two_parts(np.block([[spread(c), spread(s)], [spread(-s), spread(c)]]))
    c, s = turn(np.arange(256), np.arange(256), 256)
    both = np.stack([c, -s]).reshape(2, NZ, NQ, 2, 256).transpose(2, 1, 0, 3, 4)
    out["box_one"] = two_parts(both.reshape(512, 256))
    c, s = turn(np.arange(32), np.arange(32), 32)
    out["box_two"] = two_parts(np.block([[c, s], [-s, c]]))
    lanes = np.concatenate([np.arange(384) // 48, (np.arange(128) >> 1) & 7])
    c, s = turn(np.arange(64), lanes, 256)
    out["box_twist"] = np.stack([c, s]).astype(np.float32)
    c, s = turn(np.arange(4), lanes, 4)
    out["box_quarter"] = np.stack([c, s], axis=1).reshape(4, 2, 512).astype(np.float32)
    return out


def halves(value):
    high = value.astype(bf16)
    return high, (value - high.astype(f32)).astype(bf16)


def mm(left, right):
    return lax.dot_general(left, right, (((1,), (0,)), ((), ())), preferred_element_type=f32)


def mmt(left, right):
    return lax.dot_general(left, right, (((1,), (1,)), ((), ())), preferred_element_type=f32)


def exact_product(table_ref, value, dot):
    return dot(table_ref[0], value) + dot(table_ref[1], value)


def full_product(table_ref, value, dot):
    high, low = halves(value)
    return dot(table_ref[0], high) + (dot(table_ref[1], high) + dot(table_ref[0], low))


def place():
    rows = lax.axis_index("rows")
    half = lax.axis_index("half")
    z = rows // NQ
    q = rows - z * NQ
    return rows, half, z, q, q * NY + half


def signal(barrier, rows, half):
    pl.semaphore_signal(barrier, inc=1, device_id=(rows, half), device_id_type=MESH)


def remote(src, dst, send, recv, rows, half):
    return pltpu.make_async_remote_copy(
        src_ref=src, dst_ref=dst, send_sem=send, recv_sem=recv, device_id=(rows, half), device_id_type=MESH
    )


def wait_for(ref, sem):
    pltpu.make_async_copy(ref, ref, sem).wait()


def loop(count, body, start=0, unroll=1):
    def step(index, carry):
        body(index)
        return carry

    lax.fori_loop(start, count, step, 0, unroll=unroll)


def signal_plane(barrier, z, p):
    def greet(k):
        other = lax.rem(p + k, 32)
        signal(barrier, z * NQ + other // NY, lax.rem(other, NY))

    loop(32, greet, 1)


def far_first(count):
    return sorted(range(1, count), key=lambda k: -min(k, count - k))


def main_kernel(
    tops_ref, shift_ref, class_ref, live_ref, mic_ref, row_twist_ref, box_twist_ref, quarter_ref, col_twist_ref, box_two_ref,
    row_one_hbm, row_two_hbm, box_one_hbm, col_one_hbm, col_two_hbm, power_ref, means_ref,
    row_one_ref, row_two_ref, box_one_ref, col_one_ref, col_two_ref, band_ref, table_in, table_ref,
    boxes, boxes_in, freq, freq_mid, freq_ready, freq_in, held, to_z, landed, sums, got, early, local, load_sem, send, recv,
):
    rows, y, z, q, p = place()
    before, after = lax.rem(z + NZ - 1, NZ), lax.rem(z + 1, NZ)
    barrier = pltpu.get_barrier_semaphore()
    for k in far_first(NZ):
        signal(barrier, lax.rem(z + k, NZ) * NQ + q, y)
    loop(32, lambda k: signal(barrier, after * NQ + k // NY, lax.rem(k, NY)))
    loop(NQ, lambda k: signal(barrier, before * NQ + k, y))
    signal_plane(barrier, z, p)

    own = [pltpu.make_async_copy(shift_ref, table_in.at[p], local.at[4])]
    for a in range(4):
        own.append(pltpu.make_async_copy(mic_ref.at[:, pl.ds(256 * a, 256)], band_ref.at[NY * y + a], local.at[a]))
    for copy in own:
        copy.start()
    loads = []
    for index, (source, target) in enumerate(
        (
            (row_one_hbm, row_one_ref),
            (row_two_hbm, row_two_ref),
            (box_one_hbm, box_one_ref),
            (col_one_hbm, col_one_ref),
            (col_two_hbm, col_two_ref),
        )
    ):
        loads.append(pltpu.make_async_copy(source, target, load_sem.at[index]))
        loads[-1].start()
    for copy in own:
        copy.wait()
    pl.semaphore_wait(barrier, 15 + 63 + NQ)

    mine = band_ref.at[pl.ds(NY * y, 4)]
    for k in (2, 1, 3):
        remote(mine, mine, send.at[6], recv.at[6], rows, lax.rem(y + k, NY)).start()
    for k in range(NQ):
        remote(table_in.at[p], table_in.at[32 + q], send.at[7], recv.at[7], after * NQ + k, y).start()

    def tell(k):
        other = lax.rem(p + k, 32)
        remote(
            table_in.at[p], table_in.at[p], send.at[7], recv.at[7], z * NQ + other // NY, lax.rem(other, NY)
        ).start()

    loop(32, tell, 1)
    wait_for(table_in.at[pl.ds(0, 31 + NQ)], recv.at[7])
    to_scalar = pltpu.make_async_copy(table_in, table_ref, local.at[0])
    to_scalar.start()
    wait_for(band_ref.at[pl.ds(0, 12)], recv.at[6])
    to_scalar.wait()

    lane = lax.broadcasted_iota(jnp.int32, (32, 256), 1)

    def one_band(d):
        near = q - d
        entry = jnp.where(near >= 0, near * NY + y, 32 + near + NQ)
        home = lax.rem(rows - d + NBAND, NBAND)
        strips = []
        for s in range(4):
            left = tops_ref[(y * 4 + s) * 2 + 1, home] & 4095
            block = left >> 8
            offset = left & 255
            first = band_ref[block].astype(f32)
            second = band_ref[jnp.minimum(block + 1, 15)].astype(f32)
            picked = jnp.where(lane >= offset, first, second)
            shift = (table_ref[entry, 1, s] - offset) & 255
            strips.append(pltpu.roll(picked, shift, 1))
        boxes[:, d] = jnp.concatenate(strips, axis=0).T.reshape(32, 8, 128).astype(bf16)

    loop(REACH, one_band, unroll=3)

    here = p * REACH
    for level in range(NQ):

        @pl.when(q == level)
        def _():
            near, far = level + 1, REACH - 1 - level
            pltpu.make_async_copy(boxes.at[p, pl.ds(0, near)], boxes_in.at[pl.ds(here, near)], local.at[0]).start()
            for e in (0, 1, 3, 2):
                side = lax.rem(y + e, NY)
                group = (NY - e) % NY

                def send_both(k):
                    there = lax.rem(q + k, NQ)
                    target = there * NY + side
                    remote(
                        boxes.at[target, pl.ds(near, far)], boxes_in.at[pl.ds(here + near, far)],
                        send.at[2], recv.at[12 + group], before * NQ + there, side,
                    ).start()
                    remote(
                        boxes.at[target, pl.ds(0, near)], boxes_in.at[pl.ds(here, near)],
                        send.at[1], recv.at[8 + group], z * NQ + there, side,
                    ).start()

                def send_far_only(k):
                    there = lax.rem(q + k, NQ)
                    remote(
                        boxes.at[there * NY + side, pl.ds(near, far)], boxes_in.at[pl.ds(here + near, far)],
                        send.at[2], recv.at[12 + group], before * NQ + there, side,
                    ).start()

                loop(NQ, send_both, 1)
                if e == 0:
                    send_far_only(0)
                else:
                    send_both(0)

    loads[0].wait()
    loads[1].wait()
    real, imag = [], []
    cos_all, sin_all = row_twist_ref[y, 0], row_twist_ref[y, 1]
    for side in range(2):
        pixels = band_ref[:, :].reshape(8, 2, 32, 256)[:, side].reshape(256, 256)
        section = exact_product(row_one_ref, pixels, mm)
        cos = jnp.broadcast_to(cos_all[:, 256 * side : 256 * side + 256][:, None, :], (8, 32, 256)).reshape(256, 256)
        sin = jnp.broadcast_to(sin_all[:, 256 * side : 256 * side + 256][:, None, :], (8, 32, 256)).reshape(256, 256)
        real.append(section[:256] * cos + section[256:] * sin)
        imag.append(section[256:] * cos - section[:256] * sin)
    turned = jnp.concatenate(real + imag, axis=1)
    result = full_product(row_two_ref, turned, mmt).astype(bf16)
    freq[0] = result[:, :128]
    freq[1] = result[:, 128:]

    for k in far_first(NQ):
        other = lax.rem(q + k, NQ)
        remote(freq.at[:, pl.ds(32 * other, 32)], freq_mid.at[:, q], send.at[3], recv.at[3], z * NQ + other, y).start()
    own_mid = pltpu.make_async_copy(freq.at[:, pl.ds(32 * q, 32)], freq_mid.at[:, q], local.at[1])
    own_mid.start()
    own_mid.wait()
    wait_for(freq_mid.at[:, pl.ds(0, NQ - 1)], send.at[3])
    wait_for(freq_mid.at[:, pl.ds(0, NQ - 1)], recv.at[3])
    for h in range(2):
        freq_ready[h] = freq_mid[h].reshape(NQ, NZ, 2, 128)
    for k in far_first(NZ):
        other = lax.rem(z + k, NZ)
        remote(freq_ready.at[:, :, other], freq_in.at[:, :, z], send.at[4], recv.at[4], other * NQ + q, y).start()
    own_freq = pltpu.make_async_copy(freq_ready.at[:, :, z], freq_in.at[:, :, z], local.at[1])
    own_freq.start()

    lane = lax.broadcasted_iota(jnp.int32, (8, 128), 1)
    group = lane >> 5

    def one_home(q0, j):
        home = q0 * NY + j
        spun = []
        for d in range(REACH):
            piece = boxes_in[(((q0 + d) & 7) * NY + j) * REACH + d].astype(f32)
            spun.append([piece] + [pltpu.roll(piece, 32 * turns, 1) for turns in range(1, 4)])

        def joined(first, s):
            value = spun[first][(0 - s) % 4]
            for dd in range(1, 4):
                value = jnp.where(group == dd, spun[first + dd][(dd - s) % 4], value)
            return value

        for s in range(4):
            slot = home * 4 + s
            band = z * NQ + q0
            top = (tops_ref[(j * 4 + s) * 2, band] - band * 32) & 255
            shift = (table_ref[home, 0, s] - top) & 255
            low = jnp.where(lane >= top, joined(0, s), spun[8][(0 - s) % 4])
            held[slot] = pltpu.roll(jnp.concatenate([low, joined(4, s)], axis=1), shift, 1)

    for g in (0, 1, 3, 2):
        if g == 0:
            for level in range(NQ):

                @pl.when(q == level)
                def _():
                    wait_for(boxes_in.at[pl.ds(0, 36 - (level + 1))], recv.at[8])
                    wait_for(boxes_in.at[pl.ds(0, level + 1)], local.at[0])

        else:
            wait_for(boxes_in.at[pl.ds(0, 36)], recv.at[8 + g])
        wait_for(boxes_in.at[pl.ds(0, 36)], recv.at[12 + g])
        j = lax.rem(y + g, NY)
        loop(NQ, lambda q0: one_home(q0, j), unroll=4)

    labels = jnp.where(live_ref[...] == 1, class_ref[...], CLASSES)
    plane_labels = pltpu.roll(labels, lax.rem(NBAND - z * NQ, NBAND), 1)
    kind_lane = lax.broadcasted_iota(jnp.int32, (16, 128), 1)
    chosen = jnp.concatenate([(plane_labels[:, k : k + 1] == kind_lane).astype(f32) for k in range(NQ)], axis=0)
    chosen = chosen.T[:64].astype(bf16)
    columns = [mm(chosen, held[:, c, :].astype(bf16)) for c in range(8)]
    loads[2].wait()
    main = full_product(box_one_ref, jnp.concatenate([column[:48] for column in columns], axis=0), mmt)
    rest = full_product(box_one_ref, jnp.concatenate([column[48:50] for column in columns], axis=0), mmt)
    rest = jnp.concatenate([rest[64 * k : 64 * k + 64] for k in range(NQ)], axis=1)
    for k in range(NQ):
        for t in range(3):
            to_z[NQ * t + k] = main[64 * k : 64 * k + 64, 128 * t : 128 * t + 128].reshape(NZ, 4, 128).astype(bf16)
    to_z[24] = rest.reshape(NZ, 4, 128).astype(bf16)

    for k in far_first(NZ):
        other = lax.rem(z + k, NZ)
        remote(
            to_z.at[pl.ds(0, 16), other], landed.at[pl.ds(0, 16), z], send.at[0], recv.at[0], other * NQ + q, y
        ).start()
    for k in far_first(NZ):
        other = lax.rem(z + k, NZ)
        remote(
            to_z.at[pl.ds(16, 9), other], landed.at[pl.ds(16, 9), z], send.at[8], recv.at[16], other * NQ + q, y
        ).start()
    own = pltpu.make_async_copy(to_z.at[:, z], landed.at[:, z], local.at[2])
    own.start()

    cos_y, sin_y = quarter_ref[y, 0][None, :], quarter_ref[y, 1][None, :]
    cos = box_twist_ref[0] * cos_y - box_twist_ref[1] * sin_y
    sin = box_twist_ref[1] * cos_y + box_twist_ref[0] * sin_y

    kinds = lax.broadcasted_iota(jnp.int32, (64, 128), 0)
    counts = jnp.zeros((64, 128), f32)
    for k in range(16):
        counts = counts + (kinds == labels[k : k + 1, :]).astype(f32)
    inverse = 1.0 / (BOX * jnp.maximum(jnp.sum(counts, axis=1, keepdims=True), 1.0))

    loads[3].wait()
    loads[4].wait()
    own_freq.wait()
    wait_for(freq_in.at[:, :, pl.ds(0, NZ - 1)], send.at[4])
    wait_for(freq_in.at[:, :, pl.ds(0, NZ - 1)], recv.at[4])
    col_cos, col_sin = col_twist_ref[0], col_twist_ref[1]
    for h in range(2):
        section = exact_product(col_one_ref, freq_in[h].reshape(256, 128), mm)
        real = section[:128] * col_cos + section[128:] * col_sin
        imag = section[128:] * col_cos - section[:128] * col_sin
        result = full_product(col_two_ref, jnp.concatenate([real, imag], axis=1), mmt)
        power = (result[:128] * result[:128] + result[128:] * result[128:]) * (1.0 / (NPIX * NPIX))
        for tau in range(32):
            power_ref[0, 4 * h : 4 * h + 4, 128 * tau : 128 * tau + 128] = power[4 * tau : 4 * tau + 4]

    own.wait()
    mine = []
    for part, blocks in enumerate((pl.ds(0, 16), pl.ds(16, 9))):
        wait_for(landed.at[blocks, pl.ds(0, 15)], recv.at[16 * part])
        for t in ((0, 1), (2,))[part]:
            for k in range(NQ):
                sums[k, t] = jnp.sum(landed[NQ * t + k].astype(f32), axis=0)
        if part == 1:
            last = jnp.sum(landed[24].astype(f32), axis=0)
            for k in range(NQ):
                sums[k, 3] = last
        tiles = pl.ds(2 * part, 2)
        for k in far_first(32):
            other = lax.rem(p + k, 32)
            there = other // NY
            remote(
                sums.at[there, tiles], got.at[p, tiles], send.at[(5, 9)[part]], recv.at[(5, 17)[part]],
                z * NQ + there, lax.rem(other, NY),
            ).start()
        mine.append(pltpu.make_async_copy(sums.at[q, tiles], got.at[p, tiles], local.at[3 + part]))
        mine[-1].start()

    lanes = lax.broadcasted_iota(jnp.int32, (48, 384), 1)
    pick = (lax.rem(lanes, 48) == lax.broadcasted_iota(jnp.int32, (48, 384), 0)).astype(bf16)
    lanes = lax.broadcasted_iota(jnp.int32, (16, 128), 1)
    pick_rest = (((lanes >> 4) == q) & ((lanes & 1) == lax.broadcasted_iota(jnp.int32, (16, 128), 0))).astype(bf16)

    def turned_tiles(part):
        pieces = []
        for a in range(2):
            for t in (2 * part, 2 * part + 1):
                pieces.append(jnp.concatenate([got[:, t, a, :], got[:, t, 2 + a, :]], axis=0))
        section = full_product(box_two_ref, jnp.concatenate(pieces, axis=1), mm)
        at = slice(256 * part, 256 * part + 256)
        for a in range(2):
            real = jnp.concatenate([section[:32, 256 * a : 256 * a + 256]] * 2, axis=0)
            imag = jnp.concatenate([section[32:, 256 * a : 256 * a + 256]] * 2, axis=0)
            yield a, 0, halves(real * cos[:, at] + imag * sin[:, at])
            yield a, 1, halves(imag * cos[:, at] - real * sin[:, at])

    mine[0].wait()
    wait_for(got.at[pl.ds(0, 31), pl.ds(0, 2)], recv.at[5])
    for a, part, (high, low) in turned_tiles(0):
        early[2 * a + part] = mmt(pick[:, :256], high) + mmt(pick[:, :256], low)
    mine[1].wait()
    wait_for(got.at[pl.ds(0, 31), pl.ds(0, 2)], recv.at[17])
    for a, part, (high, low) in turned_tiles(1):
        total = mmt(pick[:, 256:], high[:, :128]) + mmt(pick[:, 256:], low[:, :128])
        means_ref[0:48, part, a, :] = (early[2 * a + part] + total) * inverse[:48]
        total = mmt(pick_rest, high[:, 128:]) + mmt(pick_rest, low[:, 128:])
        means_ref[48:50, part, a, :] = total[:2] * inverse[48:50]

    for level in range(NQ):

        @pl.when(q == level)
        def _():
            wait_for(boxes.at[pl.ds(0, 32), pl.ds(0, REACH - 1 - level)], send.at[2])
            wait_for(boxes.at[pl.ds(0, 31), pl.ds(0, level + 1)], send.at[1])

    wait_for(band_ref.at[pl.ds(0, 12)], send.at[6])
    wait_for(table_in.at[pl.ds(0, 31 + NQ)], send.at[7])
    wait_for(landed.at[pl.ds(0, 16), pl.ds(0, 15)], send.at[0])
    wait_for(landed.at[pl.ds(16, 9), pl.ds(0, 15)], send.at[8])
    wait_for(got.at[pl.ds(0, 31), pl.ds(0, 2)], send.at[5])
    wait_for(got.at[pl.ds(0, 31), pl.ds(0, 2)], send.at[9])


def call(kernel, outs, ins, out_specs, scratch=(), collective=None, name=None):
    params = dict(has_side_effects=True, collective_id=collective) if collective is not None else {}
    return pl.pallas_call(
        kernel,
        out_shape=outs,
        in_specs=ins,
        out_specs=out_specs,
        scratch_shapes=list(scratch),
        compiler_params=pltpu.CompilerParams(**params),
        name=name,
    )


def shape(*dims, dtype=bf16):
    return jax.ShapeDtypeStruct(dims, dtype)


def sems(count):
    return pltpu.SemaphoreType.DMA((count,))


def per_device(micrograph, box_tops, box_live, box_class, box_shift):
    consts = {name: jnp.asarray(value) for name, value in tables().items()}
    tops = box_tops.transpose(1, 2, 3, 0).reshape(32, NBAND)
    classes = box_class.transpose(1, 2, 0).reshape(16, NBAND)
    live = box_live.transpose(1, 2, 0).reshape(16, NBAND)
    shifts = box_shift.transpose(0, 1, 3, 2).reshape(2, 4)

    return call(
        main_kernel,
        (pltpu.VMEM((1, 8, NPIX), f32), pltpu.VMEM((CLASSES, 2, 2, 64), f32)),
        [SMEM, VMEM, VMEM, VMEM, ANY] + [VMEM] * 5 + [ANY] * 5,
        (VMEM, VMEM),
        (
            pltpu.VMEM((2, 512, 256), bf16),
            pltpu.VMEM((2, 256, 1024), bf16),
            pltpu.VMEM((2, 512, 256), bf16),
            pltpu.VMEM((2, 256, 256), bf16),
            pltpu.VMEM((2, 256, 256), bf16),
            pltpu.VMEM((16, 32, 256), bf16),
            pltpu.VMEM((32 + NQ, 2, 4), jnp.int32),
            pltpu.SMEM((32 + NQ, 2, 4), jnp.int32),
            pltpu.VMEM((32, REACH, 8, 128), bf16),
            pltpu.VMEM((32 * REACH, 8, 128), bf16),
            pltpu.VMEM((2, 256, 128), bf16),
            pltpu.VMEM((2, NQ, 32, 128), bf16),
            pltpu.VMEM((2, NQ, NZ, 2, 128), bf16),
            pltpu.VMEM((2, NQ, NZ, 2, 128), bf16),
            pltpu.VMEM((128, 8, 256), f32),
            pltpu.VMEM((25, NZ, 4, 128), bf16),
            pltpu.VMEM((25, NZ, 4, 128), bf16),
            pltpu.VMEM((NQ, 4, 4, 128), f32),
            pltpu.VMEM((32, 4, 4, 128), f32),
            pltpu.VMEM((4, 48, 64), f32),
            sems(5),
            sems(5),
            sems(10),
            sems(18),
        ),
        collective=0,
        name="main",
    )(
        tops, shifts, classes, live, micrograph, consts["row_twist"], consts["box_twist"], consts["box_quarter"], consts["col_twist"],
        consts["box_two"], consts["row_one"], consts["row_two"], consts["box_one"], consts["col_one"], consts["col_two"],
    )


def solution(mesh):
    in_specs = (P("rows", "half"), P(), P(), P(), P("rows", "half", None, None))
    out_specs = (P("half", "rows", None), P(None, None, "rows", "half"))
    return jax.shard_map(per_device, mesh=mesh, in_specs=in_specs, out_specs=out_specs, check_vma=False)
```

```python
import functools

import jax
import jax.numpy as jnp
import numpy as np
from jax import lax
from jax.experimental import pallas as pl
from jax.experimental.pallas import tpu as pltpu
from jax.sharding import PartitionSpec as P

BOX = 256
CLASSES = 50
NPIX = 4096
NZ, NQ, NY = 16, 8, 4
NBAND = 128
REACH = 9
MESH = pl.DeviceIdType.MESH
f32 = jnp.float32
bf16 = jnp.bfloat16
VMEM = pl.BlockSpec(memory_space=pltpu.VMEM)
SMEM = pl.BlockSpec(memory_space=pltpu.SMEM)
ANY = pl.BlockSpec(memory_space=pl.ANY)


def two_parts(matrix):
    high = matrix.astype(bf16)
    return np.stack([high, (matrix - high.astype(np.float64)).astype(bf16)])


def turn(left, right, length):
    angle = 2.0 * np.pi / length * np.mod(np.multiply.outer(left, right), length)
    return np.cos(angle), np.sin(angle)


@functools.lru_cache(None)
def tables():
    out = {}
    c, s = turn(np.arange(8), np.arange(8), 8)
    eye = np.eye(32)
    out["row_one"] = two_parts(np.concatenate([np.kron(c, eye), np.kron(-s, eye)]))
    angle = np.arange(8)[None] + 1024 * np.arange(4)[:, None]
    c, s = turn(angle, np.arange(512), NPIX)
    out["row_twist"] = np.stack([c, s], axis=1).astype(np.float32)
    c, s = turn(np.arange(128), np.arange(512), 512)
    real = np.concatenate([c, s], axis=1)
    imag = np.concatenate([-s, c], axis=1)
    both = np.stack([real, imag], axis=1).reshape(NZ, NQ, 2, 1024).transpose(1, 0, 2, 3)
    out["row_two"] = two_parts(both.reshape(256, 1024))
    c, s = turn(np.arange(128), np.arange(128), 128)
    real = np.stack([c, s], axis=2)
    imag = np.stack([-s, c], axis=2)
    both = np.concatenate([real, imag]).reshape(256, NZ, NQ, 2).transpose(0, 2, 1, 3)
    out["col_one"] = two_parts(both.reshape(256, 256))
    c, s = turn(np.arange(128), np.arange(32), NPIX)
    out["col_twist"] = np.stack([np.tile(c, (1, 4)), np.tile(s, (1, 4))]).astype(np.float32)
    c, s = turn(np.arange(32), np.arange(32), 32)
    same = np.eye(4)

    def spread(matrix):
        return np.einsum("tm,kl->tklm", matrix, same).reshape(128, 128)

    out["col_two"] = two_parts(np.block([[spread(c), spread(s)], [spread(-s), spread(c)]]))
    c, s = turn(np.arange(256), np.arange(256), 256)
    both = np.stack([c, -s]).reshape(2, NZ, NQ, 2, 256).transpose(2, 1, 0, 3, 4)
    out["box_one"] = two_parts(both.reshape(512, 256))
    c, s = turn(np.arange(32), np.arange(32), 32)
    out["box_two"] = two_parts(np.block([[c, s], [-s, c]]))
    lanes = np.concatenate([np.arange(384) // 48, (np.arange(128) >> 1) & 7])
    c, s = turn(np.arange(64), lanes, 256)
    out["box_twist"] = np.stack([c, s]).astype(np.float32)
    c, s = turn(np.arange(4), lanes, 4)
    out["box_quarter"] = np.stack([c, s], axis=1).reshape(4, 2, 512).astype(np.float32)
    return out


def halves(value):
    high = value.astype(bf16)
    return high, (value - high.astype(f32)).astype(bf16)


def mm(left, right):
    return lax.dot_general(left, right, (((1,), (0,)), ((), ())), preferred_element_type=f32)


def mmt(left, right):
    return lax.dot_general(left, right, (((1,), (1,)), ((), ())), preferred_element_type=f32)


def exact_product(table_ref, value, dot):
    return dot(table_ref[0], value) + dot(table_ref[1], value)


def full_product(table_ref, value, dot):
    high, low = halves(value)
    return dot(table_ref[0], high) + (dot(table_ref[1], high) + dot(table_ref[0], low))


def place():
    rows = lax.axis_index("rows")
    half = lax.axis_index("half")
    z = rows // NQ
    q = rows - z * NQ
    return rows, half, z, q, q * NY + half


def signal(barrier, rows, half):
    pl.semaphore_signal(barrier, inc=1, device_id=(rows, half), device_id_type=MESH)


def remote(src, dst, send, recv, rows, half):
    return pltpu.make_async_remote_copy(
        src_ref=src, dst_ref=dst, send_sem=send, recv_sem=recv, device_id=(rows, half), device_id_type=MESH
    )


def wait_for(ref, sem):
    pltpu.make_async_copy(ref, ref, sem).wait()


def loop(count, body, start=0, unroll=1):
    def step(index, carry):
        body(index)
        return carry

    lax.fori_loop(start, count, step, 0, unroll=unroll)


def signal_plane(barrier, z, p):
    def greet(k):
        other = lax.rem(p + k, 32)
        signal(barrier, z * NQ + other // NY, lax.rem(other, NY))

    loop(32, greet, 1)


def far_first(count):
    return sorted(range(1, count), key=lambda k: -min(k, count - k))


def main_kernel(
    mic_ref, shift_ref, tops_hbm, class_hbm, live_hbm, row_twist_hbm, box_twist_hbm, quarter_hbm, col_twist_hbm, box_two_hbm,
    row_one_hbm, row_two_hbm, box_one_hbm, col_one_hbm, col_two_hbm, power_ref, means_ref,
    tops_ref, class_ref, live_ref, row_twist_ref, box_twist_ref, quarter_ref, col_twist_ref, box_two_ref,
    row_one_ref, row_two_ref, box_one_ref, col_one_ref, col_two_ref, band_ref, table_in, table_ref, near_in, near_ref,
    boxes, boxes_in, freq, freq_mid, freq_ready, freq_in, held, to_z, landed, sums, got, early, local, load_sem, send, recv,
):
    rows, y, z, q, p = place()
    before, after = lax.rem(z + NZ - 1, NZ), lax.rem(z + 1, NZ)
    barrier = pltpu.get_barrier_semaphore()
    for k in far_first(NZ):
        signal(barrier, lax.rem(z + k, NZ) * NQ + q, y)
    loop(32, lambda k: signal(barrier, after * NQ + k // NY, lax.rem(k, NY)))
    loop(NQ, lambda k: signal(barrier, before * NQ + k, y))
    signal_plane(barrier, z, p)

    own = [
        pltpu.make_async_copy(shift_ref, table_in.at[p], local.at[4]),
        pltpu.make_async_copy(shift_ref, near_in.at[q], local.at[5]),
    ]
    for a in range(4):
        own.append(pltpu.make_async_copy(mic_ref.at[:, pl.ds(256 * a, 256)], band_ref.at[NY * y + a], local.at[a]))
    for copy in own:
        copy.start()
    loads = []
    for index, (source, target) in enumerate(
        (
            (tops_hbm, tops_ref),
            (row_twist_hbm, row_twist_ref),
            (row_one_hbm, row_one_ref),
            (row_two_hbm, row_two_ref),
            (class_hbm, class_ref),
            (live_hbm, live_ref),
            (box_one_hbm, box_one_ref),
            (quarter_hbm, quarter_ref),
            (box_twist_hbm, box_twist_ref),
            (col_twist_hbm, col_twist_ref),
            (col_one_hbm, col_one_ref),
            (col_two_hbm, col_two_ref),
            (box_two_hbm, box_two_ref),
        )
    ):
        loads.append(pltpu.make_async_copy(source, target, load_sem.at[index]))
        loads[-1].start()
    for copy in own:
        copy.wait()
    pl.semaphore_wait(barrier, 15 + 63 + NQ)

    mine = band_ref.at[pl.ds(NY * y, 4)]
    for k in (2, 1, 3):
        remote(mine, mine, send.at[6], recv.at[6], rows, lax.rem(y + k, NY)).start()
    for k in far_first(NQ):
        remote(
            near_in.at[q], near_in.at[q], send.at[10], recv.at[18], z * NQ + lax.rem(q + k, NQ), y
        ).start()
    for k in range(NQ):
        remote(near_in.at[q], near_in.at[NQ + q], send.at[10], recv.at[18], after * NQ + k, y).start()

    def tell(k):
        other = lax.rem(p + k, 32)
        remote(
            table_in.at[p], table_in.at[p], send.at[7], recv.at[7], z * NQ + other // NY, lax.rem(other, NY)
        ).start()

    loop(32, tell, 1)
    wait_for(near_in.at[pl.ds(0, 15)], recv.at[18])
    to_scalar = pltpu.make_async_copy(near_in, near_ref, local.at[0])
    to_scalar.start()
    wait_for(band_ref.at[pl.ds(0, 12)], recv.at[6])
    to_scalar.wait()
    loads[0].wait()

    lane = lax.broadcasted_iota(jnp.int32, (32, 256), 1)

    def one_band(d):
        near = q - d
        entry = jnp.where(near >= 0, near, 2 * NQ + near)
        home = lax.rem(rows - d + NBAND, NBAND)
        strips = []
        for s in range(4):
            left = tops_ref[(y * 4 + s) * 2 + 1, home] & 4095
            block = left >> 8
            offset = left & 255
            first = band_ref[block].astype(f32)
            second = band_ref[jnp.minimum(block + 1, 15)].astype(f32)
            picked = jnp.where(lane >= offset, first, second)
            shift = (near_ref[entry, 1, s] - offset) & 255
            strips.append(pltpu.roll(picked, shift, 1))
        boxes[:, d] = jnp.concatenate(strips, axis=0).T.reshape(32, 8, 128).astype(bf16)

    loop(REACH, one_band, unroll=3)

    here = p * REACH
    for level in range(NQ):

        @pl.when(q == level)
        def _():
            near, far = level + 1, REACH - 1 - level
            pltpu.make_async_copy(boxes.at[p, pl.ds(0, near)], boxes_in.at[pl.ds(here, near)], local.at[0]).start()
            for e in (0, 1, 3, 2):
                side = lax.rem(y + e, NY)
                group = (NY - e) % NY

                def send_both(k):
                    there = lax.rem(q + k, NQ)
                    target = there * NY + side
                    remote(
                        boxes.at[target, pl.ds(near, far)], boxes_in.at[pl.ds(here + near, far)],
                        send.at[2], recv.at[12 + group], before * NQ + there, side,
                    ).start()
                    remote(
                        boxes.at[target, pl.ds(0, near)], boxes_in.at[pl.ds(here, near)],
                        send.at[1], recv.at[8 + group], z * NQ + there, side,
                    ).start()

                def send_far_only(k):
                    there = lax.rem(q + k, NQ)
                    remote(
                        boxes.at[there * NY + side, pl.ds(near, far)], boxes_in.at[pl.ds(here + near, far)],
                        send.at[2], recv.at[12 + group], before * NQ + there, side,
                    ).start()

                loop(NQ, send_both, 1)
                if e == 0:
                    send_far_only(0)
                else:
                    send_both(0)

    for load in loads[1:4]:
        load.wait()
    real, imag = [], []
    cos_all, sin_all = row_twist_ref[y, 0], row_twist_ref[y, 1]
    for side in range(2):
        pixels = band_ref[:, :].reshape(8, 2, 32, 256)[:, side].reshape(256, 256)
        section = exact_product(row_one_ref, pixels, mm)
        cos = jnp.broadcast_to(cos_all[:, 256 * side : 256 * side + 256][:, None, :], (8, 32, 256)).reshape(256, 256)
        sin = jnp.broadcast_to(sin_all[:, 256 * side : 256 * side + 256][:, None, :], (8, 32, 256)).reshape(256, 256)
        real.append(section[:256] * cos + section[256:] * sin)
        imag.append(section[256:] * cos - section[:256] * sin)
    turned = jnp.concatenate(real + imag, axis=1)
    result = full_product(row_two_ref, turned, mmt).astype(bf16)
    freq[0] = result[:, :128]
    freq[1] = result[:, 128:]

    for k in far_first(NQ):
        other = lax.rem(q + k, NQ)
        remote(freq.at[:, pl.ds(32 * other, 32)], freq_mid.at[:, q], send.at[3], recv.at[3], z * NQ + other, y).start()
    own_mid = pltpu.make_async_copy(freq.at[:, pl.ds(32 * q, 32)], freq_mid.at[:, q], local.at[1])
    own_mid.start()
    own_mid.wait()
    wait_for(freq_mid.at[:, pl.ds(0, NQ - 1)], send.at[3])
    wait_for(freq_mid.at[:, pl.ds(0, NQ - 1)], recv.at[3])
    for h in range(2):
        freq_ready[h] = freq_mid[h].reshape(NQ, NZ, 2, 128)
    for k in far_first(NZ):
        other = lax.rem(z + k, NZ)
        remote(freq_ready.at[:, :, other], freq_in.at[:, :, z], send.at[4], recv.at[4], other * NQ + q, y).start()
    own_freq = pltpu.make_async_copy(freq_ready.at[:, :, z], freq_in.at[:, :, z], local.at[1])
    own_freq.start()

    wait_for(table_in.at[pl.ds(0, 31)], recv.at[7])
    to_scalar = pltpu.make_async_copy(table_in, table_ref, local.at[4])
    to_scalar.start()
    to_scalar.wait()

    lane = lax.broadcasted_iota(jnp.int32, (8, 128), 1)
    group = lane >> 5

    def one_home(q0, j):
        home = q0 * NY + j
        spun = []
        for d in range(REACH):
            piece = boxes_in[(((q0 + d) & 7) * NY + j) * REACH + d].astype(f32)
            spun.append([piece] + [pltpu.roll(piece, 32 * turns, 1) for turns in range(1, 4)])

        def joined(first, s):
            value = spun[first][(0 - s) % 4]
            for dd in range(1, 4):
                value = jnp.where(group == dd, spun[first + dd][(dd - s) % 4], value)
            return value

        for s in range(4):
            slot = home * 4 + s
            band = z * NQ + q0
            top = (tops_ref[(j * 4 + s) * 2, band] - band * 32) & 255
            shift = (table_ref[home, 0, s] - top) & 255
            low = jnp.where(lane >= top, joined(0, s), spun[8][(0 - s) % 4])
            held[slot] = pltpu.roll(jnp.concatenate([low, joined(4, s)], axis=1), shift, 1)

    for g in (0, 1, 3, 2):
        if g == 0:
            for level in range(NQ):

                @pl.when(q == level)
                def _():
                    wait_for(boxes_in.at[pl.ds(0, 36 - (level + 1))], recv.at[8])
                    wait_for(boxes_in.at[pl.ds(0, level + 1)], local.at[0])

        else:
            wait_for(boxes_in.at[pl.ds(0, 36)], recv.at[8 + g])
        wait_for(boxes_in.at[pl.ds(0, 36)], recv.at[12 + g])
        j = lax.rem(y + g, NY)
        loop(NQ, lambda q0: one_home(q0, j), unroll=4)

    for load in loads[4:7]:
        load.wait()
    labels = jnp.where(live_ref[...] == 1, class_ref[...], CLASSES)
    plane_labels = pltpu.roll(labels, lax.rem(NBAND - z * NQ, NBAND), 1)
    kind_lane = lax.broadcasted_iota(jnp.int32, (16, 128), 1)
    chosen = jnp.concatenate([(plane_labels[:, k : k + 1] == kind_lane).astype(f32) for k in range(NQ)], axis=0)
    chosen = chosen.T[:64].astype(bf16)
    columns = [mm(chosen, held[:, c, :].astype(bf16)) for c in range(8)]
    main = full_product(box_one_ref, jnp.concatenate([column[:48] for column in columns], axis=0), mmt)
    rest = full_product(box_one_ref, jnp.concatenate([column[48:50] for column in columns], axis=0), mmt)
    rest = jnp.concatenate([rest[64 * k : 64 * k + 64] for k in range(NQ)], axis=1)
    for k in range(NQ):
        for t in range(3):
            to_z[NQ * t + k] = main[64 * k : 64 * k + 64, 128 * t : 128 * t + 128].reshape(NZ, 4, 128).astype(bf16)
    to_z[24] = rest.reshape(NZ, 4, 128).astype(bf16)

    for k in far_first(NZ):
        other = lax.rem(z + k, NZ)
        remote(
            to_z.at[pl.ds(0, 16), other], landed.at[pl.ds(0, 16), z], send.at[0], recv.at[0], other * NQ + q, y
        ).start()
    for k in far_first(NZ):
        other = lax.rem(z + k, NZ)
        remote(
            to_z.at[pl.ds(16, 9), other], landed.at[pl.ds(16, 9), z], send.at[8], recv.at[16], other * NQ + q, y
        ).start()
    own = pltpu.make_async_copy(to_z.at[:, z], landed.at[:, z], local.at[2])
    own.start()

    for load in loads[7:]:
        load.wait()
    cos_y, sin_y = quarter_ref[y, 0][None, :], quarter_ref[y, 1][None, :]
    cos = box_twist_ref[0] * cos_y - box_twist_ref[1] * sin_y
    sin = box_twist_ref[1] * cos_y + box_twist_ref[0] * sin_y

    kinds = lax.broadcasted_iota(jnp.int32, (64, 128), 0)
    counts = jnp.zeros((64, 128), f32)
    for k in range(16):
        counts = counts + (kinds == labels[k : k + 1, :]).astype(f32)
    inverse = 1.0 / (BOX * jnp.maximum(jnp.sum(counts, axis=1, keepdims=True), 1.0))

    own_freq.wait()
    wait_for(freq_in.at[:, :, pl.ds(0, NZ - 1)], send.at[4])
    wait_for(freq_in.at[:, :, pl.ds(0, NZ - 1)], recv.at[4])
    col_cos, col_sin = col_twist_ref[0], col_twist_ref[1]
    for h in range(2):
        section = exact_product(col_one_ref, freq_in[h].reshape(256, 128), mm)
        real = section[:128] * col_cos + section[128:] * col_sin
        imag = section[128:] * col_cos - section[:128] * col_sin
        result = full_product(col_two_ref, jnp.concatenate([real, imag], axis=1), mmt)
        power = (result[:128] * result[:128] + result[128:] * result[128:]) * (1.0 / (NPIX * NPIX))
        for tau in range(32):
            power_ref[0, 4 * h : 4 * h + 4, 128 * tau : 128 * tau + 128] = power[4 * tau : 4 * tau + 4]

    own.wait()
    mine = []
    for part, blocks in enumerate((pl.ds(0, 16), pl.ds(16, 9))):
        wait_for(landed.at[blocks, pl.ds(0, 15)], recv.at[16 * part])
        for t in ((0, 1), (2,))[part]:
            for k in range(NQ):
                sums[k, t] = jnp.sum(landed[NQ * t + k].astype(f32), axis=0)
        if part == 1:
            last = jnp.sum(landed[24].astype(f32), axis=0)
            for k in range(NQ):
                sums[k, 3] = last
        tiles = pl.ds(2 * part, 2)
        for k in far_first(32):
            other = lax.rem(p + k, 32)
            there = other // NY
            remote(
                sums.at[there, tiles], got.at[p, tiles], send.at[(5, 9)[part]], recv.at[(5, 17)[part]],
                z * NQ + there, lax.rem(other, NY),
            ).start()
        mine.append(pltpu.make_async_copy(sums.at[q, tiles], got.at[p, tiles], local.at[3 + part]))
        mine[-1].start()

    lanes = lax.broadcasted_iota(jnp.int32, (48, 384), 1)
    pick = (lax.rem(lanes, 48) == lax.broadcasted_iota(jnp.int32, (48, 384), 0)).astype(bf16)
    lanes = lax.broadcasted_iota(jnp.int32, (16, 128), 1)
    pick_rest = (((lanes >> 4) == q) & ((lanes & 1) == lax.broadcasted_iota(jnp.int32, (16, 128), 0))).astype(bf16)

    def turned_tiles(part):
        pieces = []
        for a in range(2):
            for t in (2 * part, 2 * part + 1):
                pieces.append(jnp.concatenate([got[:, t, a, :], got[:, t, 2 + a, :]], axis=0))
        section = full_product(box_two_ref, jnp.concatenate(pieces, axis=1), mm)
        at = slice(256 * part, 256 * part + 256)
        for a in range(2):
            real = jnp.concatenate([section[:32, 256 * a : 256 * a + 256]] * 2, axis=0)
            imag = jnp.concatenate([section[32:, 256 * a : 256 * a + 256]] * 2, axis=0)
            yield a, 0, halves(real * cos[:, at] + imag * sin[:, at])
            yield a, 1, halves(imag * cos[:, at] - real * sin[:, at])

    mine[0].wait()
    wait_for(got.at[pl.ds(0, 31), pl.ds(0, 2)], recv.at[5])
    for a, part, (high, low) in turned_tiles(0):
        early[2 * a + part] = mmt(pick[:, :256], high) + mmt(pick[:, :256], low)
    mine[1].wait()
    wait_for(got.at[pl.ds(0, 31), pl.ds(0, 2)], recv.at[17])
    for a, part, (high, low) in turned_tiles(1):
        total = mmt(pick[:, 256:], high[:, :128]) + mmt(pick[:, 256:], low[:, :128])
        means_ref[0:48, part, a, :] = (early[2 * a + part] + total) * inverse[:48]
        total = mmt(pick_rest, high[:, 128:]) + mmt(pick_rest, low[:, 128:])
        means_ref[48:50, part, a, :] = total[:2] * inverse[48:50]

    for level in range(NQ):

        @pl.when(q == level)
        def _():
            wait_for(boxes.at[pl.ds(0, 32), pl.ds(0, REACH - 1 - level)], send.at[2])
            wait_for(boxes.at[pl.ds(0, 31), pl.ds(0, level + 1)], send.at[1])

    wait_for(band_ref.at[pl.ds(0, 12)], send.at[6])
    wait_for(table_in.at[pl.ds(0, 31)], send.at[7])
    wait_for(near_in.at[pl.ds(0, 15)], send.at[10])
    wait_for(landed.at[pl.ds(0, 16), pl.ds(0, 15)], send.at[0])
    wait_for(landed.at[pl.ds(16, 9), pl.ds(0, 15)], send.at[8])
    wait_for(got.at[pl.ds(0, 31), pl.ds(0, 2)], send.at[5])
    wait_for(got.at[pl.ds(0, 31), pl.ds(0, 2)], send.at[9])


def call(kernel, outs, ins, out_specs, scratch=(), collective=None, name=None):
    params = dict(has_side_effects=True, collective_id=collective) if collective is not None else {}
    return pl.pallas_call(
        kernel,
        out_shape=outs,
        in_specs=ins,
        out_specs=out_specs,
        scratch_shapes=list(scratch),
        compiler_params=pltpu.CompilerParams(**params),
        name=name,
    )


def shape(*dims, dtype=bf16):
    return jax.ShapeDtypeStruct(dims, dtype)


def sems(count):
    return pltpu.SemaphoreType.DMA((count,))


def per_device(micrograph, box_tops, box_live, box_class, box_shift):
    consts = {name: jnp.asarray(value) for name, value in tables().items()}
    tops = box_tops.transpose(1, 2, 3, 0).reshape(32, NBAND)
    classes = box_class.transpose(1, 2, 0).reshape(16, NBAND)
    live = box_live.transpose(1, 2, 0).reshape(16, NBAND)
    shifts = box_shift.transpose(0, 1, 3, 2).reshape(2, 4)

    return call(
        main_kernel,
        (pltpu.VMEM((1, 8, NPIX), f32), pltpu.VMEM((CLASSES, 2, 2, 64), f32)),
        [ANY] * 15,
        (VMEM, VMEM),
        (
            pltpu.SMEM((32, NBAND), jnp.int32),
            pltpu.VMEM((16, NBAND), jnp.int32),
            pltpu.VMEM((16, NBAND), jnp.int32),
            pltpu.VMEM((4, 2, 8, 512), f32),
            pltpu.VMEM((2, 64, 512), f32),
            pltpu.VMEM((4, 2, 512), f32),
            pltpu.VMEM((2, 128, 128), f32),
            pltpu.VMEM((2, 64, 64), bf16),
            pltpu.VMEM((2, 512, 256), bf16),
            pltpu.VMEM((2, 256, 1024), bf16),
            pltpu.VMEM((2, 512, 256), bf16),
            pltpu.VMEM((2, 256, 256), bf16),
            pltpu.VMEM((2, 256, 256), bf16),
            pltpu.VMEM((16, 32, 256), bf16),
            pltpu.VMEM((32, 2, 4), jnp.int32),
            pltpu.SMEM((32, 2, 4), jnp.int32),
            pltpu.VMEM((2 * NQ, 2, 4), jnp.int32),
            pltpu.SMEM((2 * NQ, 2, 4), jnp.int32),
            pltpu.VMEM((32, REACH, 8, 128), bf16),
            pltpu.VMEM((32 * REACH, 8, 128), bf16),
            pltpu.VMEM((2, 256, 128), bf16),
            pltpu.VMEM((2, NQ, 32, 128), bf16),
            pltpu.VMEM((2, NQ, NZ, 2, 128), bf16),
            pltpu.VMEM((2, NQ, NZ, 2, 128), bf16),
            pltpu.VMEM((128, 8, 256), f32),
            pltpu.VMEM((25, NZ, 4, 128), bf16),
            pltpu.VMEM((25, NZ, 4, 128), bf16),
            pltpu.VMEM((NQ, 4, 4, 128), f32),
            pltpu.VMEM((32, 4, 4, 128), f32),
            pltpu.VMEM((4, 48, 64), f32),
            sems(6),
            sems(13),
            sems(11),
            sems(19),
        ),
        collective=0,
        name="main",
    )(
        micrograph, shifts, tops, classes, live, consts["row_twist"], consts["box_twist"], consts["box_quarter"], consts["col_twist"],
        consts["box_two"], consts["row_one"], consts["row_two"], consts["box_one"], consts["col_one"], consts["col_two"],
    )


def solution(mesh):
    in_specs = (P("rows", "half"), P(), P(), P(), P("rows", "half", None, None))
    out_specs = (P("half", "rows", None), P(None, None, "rows", "half"))
    return jax.shard_map(per_device, mesh=mesh, in_specs=in_specs, out_specs=out_specs, check_vma=False)
```

```python
import functools

import jax
import jax.numpy as jnp
import numpy as np
from jax import lax
from jax.experimental import pallas as pl
from jax.experimental.pallas import tpu as pltpu
from jax.sharding import PartitionSpec as P

BOX = 256
CLASSES = 50
NPIX = 4096
NZ, NQ, NY = 16, 8, 4
NBAND = 128
REACH = 9
MESH = pl.DeviceIdType.MESH
f32 = jnp.float32
bf16 = jnp.bfloat16
VMEM = pl.BlockSpec(memory_space=pltpu.VMEM)
SMEM = pl.BlockSpec(memory_space=pltpu.SMEM)
ANY = pl.BlockSpec(memory_space=pl.ANY)


def two_parts(matrix):
    high = matrix.astype(bf16)
    return np.stack([high, (matrix - high.astype(np.float64)).astype(bf16)])


def turn(left, right, length):
    angle = 2.0 * np.pi / length * np.mod(np.multiply.outer(left, right), length)
    return np.cos(angle), np.sin(angle)


@functools.lru_cache(None)
def tables():
    out = {}
    c, s = turn(np.arange(8), np.arange(8), 8)
    eye = np.eye(32)
    out["row_one"] = two_parts(np.concatenate([np.kron(c, eye), np.kron(-s, eye)]))
    angle = np.arange(8)[None] + 1024 * np.arange(4)[:, None]
    c, s = turn(angle, np.arange(512), NPIX)
    out["row_twist"] = np.stack([c, s], axis=1).astype(np.float32)
    c, s = turn(np.arange(128), np.arange(512), 512)
    real = np.concatenate([c, s], axis=1)
    imag = np.concatenate([-s, c], axis=1)
    both = np.stack([real, imag], axis=1).reshape(NZ, NQ, 2, 1024).transpose(1, 0, 2, 3)
    out["row_two"] = two_parts(both.reshape(256, 1024))
    c, s = turn(np.arange(128), np.arange(128), 128)
    real = np.stack([c, s], axis=2)
    imag = np.stack([-s, c], axis=2)
    both = np.concatenate([real, imag]).reshape(256, NZ, NQ, 2).transpose(0, 2, 1, 3)
    out["col_one"] = two_parts(both.reshape(256, 256))
    c, s = turn(np.arange(128), np.arange(32), NPIX)
    out["col_twist"] = np.stack([np.tile(c, (1, 4)), np.tile(s, (1, 4))]).astype(np.float32)
    c, s = turn(np.arange(32), np.arange(32), 32)
    same = np.eye(4)

    def spread(matrix):
        return np.einsum("tm,kl->tklm", matrix, same).reshape(128, 128)

    out["col_two"] = two_parts(np.block([[spread(c), spread(s)], [spread(-s), spread(c)]]))
    c, s = turn(np.arange(256), np.arange(256), 256)
    both = np.stack([c, -s]).reshape(2, NZ, NQ, 2, 256).transpose(2, 1, 0, 3, 4)
    out["box_one"] = two_parts(both.reshape(512, 256))
    c, s = turn(np.arange(32), np.arange(32), 32)
    out["box_two"] = two_parts(np.block([[c, s], [-s, c]]))
    lanes = np.concatenate([np.arange(384) // 48, (np.arange(128) >> 1) & 7])
    c, s = turn(np.arange(64), lanes, 256)
    out["box_twist"] = np.stack([c, s]).astype(np.float32)
    c, s = turn(np.arange(4), lanes, 4)
    out["box_quarter"] = np.stack([c, s], axis=1).reshape(4, 2, 512).astype(np.float32)
    return out


def halves(value):
    high = value.astype(bf16)
    return high, (value - high.astype(f32)).astype(bf16)


def mm(left, right):
    return lax.dot_general(left, right, (((1,), (0,)), ((), ())), preferred_element_type=f32)


def mmt(left, right):
    return lax.dot_general(left, right, (((1,), (1,)), ((), ())), preferred_element_type=f32)


def exact_product(table_ref, value, dot):
    return dot(table_ref[0], value) + dot(table_ref[1], value)


def full_product(table_ref, value, dot):
    high, low = halves(value)
    return dot(table_ref[0], high) + (dot(table_ref[1], high) + dot(table_ref[0], low))


def place():
    rows = lax.axis_index("rows")
    half = lax.axis_index("half")
    z = rows // NQ
    q = rows - z * NQ
    return rows, half, z, q, q * NY + half


def signal(barrier, rows, half):
    pl.semaphore_signal(barrier, inc=1, device_id=(rows, half), device_id_type=MESH)


def remote(src, dst, send, recv, rows, half):
    return pltpu.make_async_remote_copy(
        src_ref=src, dst_ref=dst, send_sem=send, recv_sem=recv, device_id=(rows, half), device_id_type=MESH
    )


def wait_for(ref, sem):
    pltpu.make_async_copy(ref, ref, sem).wait()


def loop(count, body, start=0, unroll=1):
    def step(index, carry):
        body(index)
        return carry

    lax.fori_loop(start, count, step, 0, unroll=unroll)


def signal_plane(barrier, z, p):
    def greet(k):
        other = lax.rem(p + k, 32)
        signal(barrier, z * NQ + other // NY, lax.rem(other, NY))

    loop(32, greet, 1)


def far_first(count):
    return sorted(range(1, count), key=lambda k: -min(k, count - k))


def main_kernel(
    mic_ref, shift_ref, tops_hbm, class_hbm, live_hbm, row_twist_hbm, box_twist_hbm, quarter_hbm, col_twist_hbm, box_two_hbm,
    row_one_hbm, row_two_hbm, box_one_hbm, col_one_hbm, col_two_hbm, power_ref, means_ref,
    tops_ref, class_ref, live_ref, row_twist_ref, box_twist_ref, quarter_ref, col_twist_ref, box_two_ref,
    row_one_ref, row_two_ref, box_one_ref, col_one_ref, col_two_ref, band_ref, table_in, table_ref, near_in, near_ref,
    boxes, boxes_in, freq, freq_mid, freq_ready, freq_in, held, to_z, landed, sums, got, early, local, load_sem, send, recv,
):
    rows, y, z, q, p = place()
    before, after = lax.rem(z + NZ - 1, NZ), lax.rem(z + 1, NZ)
    barrier = pltpu.get_barrier_semaphore()
    for k in far_first(NZ):
        signal(barrier, lax.rem(z + k, NZ) * NQ + q, y)
    loop(32, lambda k: signal(barrier, after * NQ + k // NY, lax.rem(k, NY)))
    loop(NQ, lambda k: signal(barrier, before * NQ + k, y))
    signal_plane(barrier, z, p)

    own = [
        pltpu.make_async_copy(shift_ref, table_in.at[p], local.at[4]),
        pltpu.make_async_copy(shift_ref, near_in.at[q], local.at[5]),
    ]
    for a in range(4):
        own.append(pltpu.make_async_copy(mic_ref.at[:, pl.ds(256 * a, 256)], band_ref.at[NY * y + a], local.at[a]))
    for copy in own:
        copy.start()
    loads = []
    for index, (source, target) in enumerate(
        (
            (tops_hbm, tops_ref),
            (row_twist_hbm, row_twist_ref),
            (row_one_hbm, row_one_ref),
            (row_two_hbm, row_two_ref),
            (class_hbm, class_ref),
            (live_hbm, live_ref),
            (box_one_hbm, box_one_ref),
            (quarter_hbm, quarter_ref),
            (box_twist_hbm, box_twist_ref),
            (col_twist_hbm, col_twist_ref),
            (col_one_hbm, col_one_ref),
            (col_two_hbm, col_two_ref),
            (box_two_hbm, box_two_ref),
        )
    ):
        loads.append(pltpu.make_async_copy(source, target, load_sem.at[index]))
        loads[-1].start()
    for copy in own:
        copy.wait()
    pl.semaphore_wait(barrier, 15 + 63 + NQ)

    mine = band_ref.at[pl.ds(NY * y, 4)]
    for k in (2, 1, 3):
        remote(mine, mine, send.at[6], recv.at[6], rows, lax.rem(y + k, NY)).start()
    for k in far_first(NQ):
        remote(
            near_in.at[q], near_in.at[q], send.at[10], recv.at[18], z * NQ + lax.rem(q + k, NQ), y
        ).start()
    for k in range(NQ):
        remote(near_in.at[q], near_in.at[NQ + q], send.at[10], recv.at[18], after * NQ + k, y).start()

    def tell(k):
        other = lax.rem(p + k, 32)
        remote(
            table_in.at[p], table_in.at[p], send.at[7], recv.at[7], z * NQ + other // NY, lax.rem(other, NY)
        ).start()

    loop(32, tell, 1)
    wait_for(near_in.at[pl.ds(0, 15)], recv.at[18])
    to_scalar = pltpu.make_async_copy(near_in, near_ref, local.at[0])
    to_scalar.start()
    wait_for(band_ref.at[pl.ds(0, 12)], recv.at[6])
    to_scalar.wait()
    loads[0].wait()

    lane = lax.broadcasted_iota(jnp.int32, (32, 256), 1)

    def one_band(d):
        near = q - d
        entry = jnp.where(near >= 0, near, 2 * NQ + near)
        home = lax.rem(rows - d + NBAND, NBAND)
        strips = []
        for s in range(4):
            left = tops_ref[(y * 4 + s) * 2 + 1, home] & 4095
            block = left >> 8
            offset = left & 255
            first = band_ref[block].astype(f32)
            second = band_ref[jnp.minimum(block + 1, 15)].astype(f32)
            picked = jnp.where(lane >= offset, first, second)
            shift = (near_ref[entry, 1, s] - offset) & 255
            strips.append(pltpu.roll(picked, shift, 1))
        boxes[:, d] = jnp.concatenate(strips, axis=0).T.reshape(32, 8, 128).astype(bf16)

    loop(REACH, one_band, unroll=3)

    here = p * REACH
    for level in range(NQ):

        @pl.when(q == level)
        def _():
            near, far = level + 1, REACH - 1 - level
            pltpu.make_async_copy(boxes.at[p, pl.ds(0, near)], boxes_in.at[pl.ds(here, near)], local.at[0]).start()
            for e in (0, 1, 3, 2):
                side = lax.rem(y + e, NY)
                group = (NY - e) % NY

                def send_both(k):
                    there = lax.rem(q + k, NQ)
                    target = there * NY + side
                    remote(
                        boxes.at[target, pl.ds(near, far)], boxes_in.at[pl.ds(here + near, far)],
                        send.at[2], recv.at[12 + group], before * NQ + there, side,
                    ).start()
                    remote(
                        boxes.at[target, pl.ds(0, near)], boxes_in.at[pl.ds(here, near)],
                        send.at[1], recv.at[8 + group], z * NQ + there, side,
                    ).start()

                def send_far_only(k):
                    there = lax.rem(q + k, NQ)
                    remote(
                        boxes.at[there * NY + side, pl.ds(near, far)], boxes_in.at[pl.ds(here + near, far)],
                        send.at[2], recv.at[12 + group], before * NQ + there, side,
                    ).start()

                loop(NQ, send_both, 1)
                if e == 0:
                    send_far_only(0)
                else:
                    send_both(0)

    for load in loads[1:4]:
        load.wait()
    real, imag = [], []
    cos_all, sin_all = row_twist_ref[y, 0], row_twist_ref[y, 1]
    for side in range(2):
        pixels = band_ref[:, :].reshape(8, 2, 32, 256)[:, side].reshape(256, 256)
        section = exact_product(row_one_ref, pixels, mm)
        cos = jnp.broadcast_to(cos_all[:, 256 * side : 256 * side + 256][:, None, :], (8, 32, 256)).reshape(256, 256)
        sin = jnp.broadcast_to(sin_all[:, 256 * side : 256 * side + 256][:, None, :], (8, 32, 256)).reshape(256, 256)
        real.append(section[:256] * cos + section[256:] * sin)
        imag.append(section[256:] * cos - section[:256] * sin)
    turned = jnp.concatenate(real + imag, axis=1)
    result = full_product(row_two_ref, turned, mmt).astype(bf16)
    freq[0] = result[:, :128]
    freq[1] = result[:, 128:]

    for k in far_first(NQ):
        other = lax.rem(q + k, NQ)
        remote(freq.at[:, pl.ds(32 * other, 32)], freq_mid.at[:, q], send.at[3], recv.at[3], z * NQ + other, y).start()
    own_mid = pltpu.make_async_copy(freq.at[:, pl.ds(32 * q, 32)], freq_mid.at[:, q], local.at[1])
    own_mid.start()
    own_mid.wait()
    wait_for(freq_mid.at[:, pl.ds(0, NQ - 1)], send.at[3])
    wait_for(freq_mid.at[:, pl.ds(0, NQ - 1)], recv.at[3])
    for h in range(2):
        freq_ready[h] = freq_mid[h].reshape(NQ, NZ, 2, 128)
    for k in far_first(NZ):
        other = lax.rem(z + k, NZ)
        remote(freq_ready.at[:, :, other], freq_in.at[:, :, z], send.at[4], recv.at[4], other * NQ + q, y).start()
    own_freq = pltpu.make_async_copy(freq_ready.at[:, :, z], freq_in.at[:, :, z], local.at[1])
    own_freq.start()

    wait_for(table_in.at[pl.ds(0, 31)], recv.at[7])
    to_scalar = pltpu.make_async_copy(table_in, table_ref, local.at[4])
    to_scalar.start()
    to_scalar.wait()

    lane = lax.broadcasted_iota(jnp.int32, (8, 128), 1)
    group = lane >> 5

    def one_home(q0, j):
        home = q0 * NY + j
        spun = []
        for d in range(REACH):
            piece = boxes_in[(((q0 + d) & 7) * NY + j) * REACH + d].astype(f32)
            spun.append([piece] + [pltpu.roll(piece, 32 * turns, 1) for turns in range(1, 4)])

        def joined(first, s):
            value = spun[first][(0 - s) % 4]
            for dd in range(1, 4):
                value = jnp.where(group == dd, spun[first + dd][(dd - s) % 4], value)
            return value

        for s in range(4):
            slot = home * 4 + s
            band = z * NQ + q0
            top = (tops_ref[(j * 4 + s) * 2, band] - band * 32) & 255
            shift = (table_ref[home, 0, s] - top) & 255
            low = jnp.where(lane >= top, joined(0, s), spun[8][(0 - s) % 4])
            held[slot] = pltpu.roll(jnp.concatenate([low, joined(4, s)], axis=1), shift, 1)

    for g in (0, 1, 3, 2):
        if g == 0:
            for level in range(NQ):

                @pl.when(q == level)
                def _():
                    wait_for(boxes_in.at[pl.ds(0, 36 - (level + 1))], recv.at[8])
                    wait_for(boxes_in.at[pl.ds(0, level + 1)], local.at[0])

        else:
            wait_for(boxes_in.at[pl.ds(0, 36)], recv.at[8 + g])
        wait_for(boxes_in.at[pl.ds(0, 36)], recv.at[12 + g])
        j = lax.rem(y + g, NY)
        loop(NQ, lambda q0: one_home(q0, j), unroll=4)

    for load in loads[4:7]:
        load.wait()
    labels = jnp.where(live_ref[...] == 1, class_ref[...], CLASSES)
    plane_labels = pltpu.roll(labels, lax.rem(NBAND - z * NQ, NBAND), 1)
    kind_lane = lax.broadcasted_iota(jnp.int32, (16, 128), 1)
    chosen = jnp.concatenate([(plane_labels[:, k : k + 1] == kind_lane).astype(f32) for k in range(NQ)], axis=0)
    chosen = chosen.T[:64].astype(bf16)
    columns = [mm(chosen, held[:, c, :].astype(bf16)) for c in range(8)]
    main = full_product(box_one_ref, jnp.concatenate([column[:48] for column in columns], axis=0), mmt)
    for t in range(2):
        for k in range(NQ):
            to_z[NQ * t + k] = main[64 * k : 64 * k + 64, 128 * t : 128 * t + 128].reshape(NZ, 4, 128).astype(bf16)
    for k in far_first(NZ):
        other = lax.rem(z + k, NZ)
        remote(
            to_z.at[pl.ds(0, 16), other], landed.at[pl.ds(0, 16), z], send.at[0], recv.at[0], other * NQ + q, y
        ).start()
    for k in range(NQ):
        to_z[2 * NQ + k] = main[64 * k : 64 * k + 64, 256:384].reshape(NZ, 4, 128).astype(bf16)
    rest = full_product(box_one_ref, jnp.concatenate([column[48:50] for column in columns], axis=0), mmt)
    rest = jnp.concatenate([rest[64 * k : 64 * k + 64] for k in range(NQ)], axis=1)
    to_z[24] = rest.reshape(NZ, 4, 128).astype(bf16)
    for k in far_first(NZ):
        other = lax.rem(z + k, NZ)
        remote(
            to_z.at[pl.ds(16, 9), other], landed.at[pl.ds(16, 9), z], send.at[8], recv.at[16], other * NQ + q, y
        ).start()
    own = pltpu.make_async_copy(to_z.at[:, z], landed.at[:, z], local.at[2])
    own.start()

    for load in loads[7:]:
        load.wait()
    cos_y, sin_y = quarter_ref[y, 0][None, :], quarter_ref[y, 1][None, :]
    cos = box_twist_ref[0] * cos_y - box_twist_ref[1] * sin_y
    sin = box_twist_ref[1] * cos_y + box_twist_ref[0] * sin_y

    kinds = lax.broadcasted_iota(jnp.int32, (64, 128), 0)
    counts = jnp.zeros((64, 128), f32)
    for k in range(16):
        counts = counts + (kinds == labels[k : k + 1, :]).astype(f32)
    inverse = 1.0 / (BOX * jnp.maximum(jnp.sum(counts, axis=1, keepdims=True), 1.0))

    own_freq.wait()
    wait_for(freq_in.at[:, :, pl.ds(0, NZ - 1)], send.at[4])
    wait_for(freq_in.at[:, :, pl.ds(0, NZ - 1)], recv.at[4])
    col_cos, col_sin = col_twist_ref[0], col_twist_ref[1]
    for h in range(2):
        section = exact_product(col_one_ref, freq_in[h].reshape(256, 128), mm)
        real = section[:128] * col_cos + section[128:] * col_sin
        imag = section[128:] * col_cos - section[:128] * col_sin
        result = full_product(col_two_ref, jnp.concatenate([real, imag], axis=1), mmt)
        power = (result[:128] * result[:128] + result[128:] * result[128:]) * (1.0 / (NPIX * NPIX))
        for tau in range(32):
            power_ref[0, 4 * h : 4 * h + 4, 128 * tau : 128 * tau + 128] = power[4 * tau : 4 * tau + 4]

    own.wait()
    mine = []
    for part, blocks in enumerate((pl.ds(0, 16), pl.ds(16, 9))):
        wait_for(landed.at[blocks, pl.ds(0, 15)], recv.at[16 * part])
        for t in ((0, 1), (2,))[part]:
            for k in range(NQ):
                sums[k, t] = jnp.sum(landed[NQ * t + k].astype(f32), axis=0)
        if part == 1:
            last = jnp.sum(landed[24].astype(f32), axis=0)
            for k in range(NQ):
                sums[k, 3] = last
        tiles = pl.ds(2 * part, 2)
        for k in far_first(32):
            other = lax.rem(p + k, 32)
            there = other // NY
            remote(
                sums.at[there, tiles], got.at[p, tiles], send.at[(5, 9)[part]], recv.at[(5, 17)[part]],
                z * NQ + there, lax.rem(other, NY),
            ).start()
        mine.append(pltpu.make_async_copy(sums.at[q, tiles], got.at[p, tiles], local.at[3 + part]))
        mine[-1].start()

    lanes = lax.broadcasted_iota(jnp.int32, (48, 384), 1)
    pick = (lax.rem(lanes, 48) == lax.broadcasted_iota(jnp.int32, (48, 384), 0)).astype(bf16)
    lanes = lax.broadcasted_iota(jnp.int32, (16, 128), 1)
    pick_rest = (((lanes >> 4) == q) & ((lanes & 1) == lax.broadcasted_iota(jnp.int32, (16, 128), 0))).astype(bf16)

    def turned_tiles(part):
        pieces = []
        for a in range(2):
            for t in (2 * part, 2 * part + 1):
                pieces.append(jnp.concatenate([got[:, t, a, :], got[:, t, 2 + a, :]], axis=0))
        section = full_product(box_two_ref, jnp.concatenate(pieces, axis=1), mm)
        at = slice(256 * part, 256 * part + 256)
        for a in range(2):
            real = jnp.concatenate([section[:32, 256 * a : 256 * a + 256]] * 2, axis=0)
            imag = jnp.concatenate([section[32:, 256 * a : 256 * a + 256]] * 2, axis=0)
            yield a, 0, halves(real * cos[:, at] + imag * sin[:, at])
            yield a, 1, halves(imag * cos[:, at] - real * sin[:, at])

    mine[0].wait()
    wait_for(got.at[pl.ds(0, 31), pl.ds(0, 2)], recv.at[5])
    for a, part, (high, low) in turned_tiles(0):
        early[2 * a + part] = mmt(pick[:, :256], high) + mmt(pick[:, :256], low)
    mine[1].wait()
    wait_for(got.at[pl.ds(0, 31), pl.ds(0, 2)], recv.at[17])
    for a, part, (high, low) in turned_tiles(1):
        total = mmt(pick[:, 256:], high[:, :128]) + mmt(pick[:, 256:], low[:, :128])
        means_ref[0:48, part, a, :] = (early[2 * a + part] + total) * inverse[:48]
        total = mmt(pick_rest, high[:, 128:]) + mmt(pick_rest, low[:, 128:])
        means_ref[48:50, part, a, :] = total[:2] * inverse[48:50]

    for level in range(NQ):

        @pl.when(q == level)
        def _():
            wait_for(boxes.at[pl.ds(0, 32), pl.ds(0, REACH - 1 - level)], send.at[2])
            wait_for(boxes.at[pl.ds(0, 31), pl.ds(0, level + 1)], send.at[1])

    wait_for(band_ref.at[pl.ds(0, 12)], send.at[6])
    wait_for(table_in.at[pl.ds(0, 31)], send.at[7])
    wait_for(near_in.at[pl.ds(0, 15)], send.at[10])
    wait_for(landed.at[pl.ds(0, 16), pl.ds(0, 15)], send.at[0])
    wait_for(landed.at[pl.ds(16, 9), pl.ds(0, 15)], send.at[8])
    wait_for(got.at[pl.ds(0, 31), pl.ds(0, 2)], send.at[5])
    wait_for(got.at[pl.ds(0, 31), pl.ds(0, 2)], send.at[9])


def call(kernel, outs, ins, out_specs, scratch=(), collective=None, name=None):
    params = dict(has_side_effects=True, collective_id=collective) if collective is not None else {}
    return pl.pallas_call(
        kernel,
        out_shape=outs,
        in_specs=ins,
        out_specs=out_specs,
        scratch_shapes=list(scratch),
        compiler_params=pltpu.CompilerParams(**params),
        name=name,
    )


def shape(*dims, dtype=bf16):
    return jax.ShapeDtypeStruct(dims, dtype)


def sems(count):
    return pltpu.SemaphoreType.DMA((count,))


def per_device(micrograph, box_tops, box_live, box_class, box_shift):
    consts = {name: jnp.asarray(value) for name, value in tables().items()}
    tops = box_tops.transpose(1, 2, 3, 0).reshape(32, NBAND)
    classes = box_class.transpose(1, 2, 0).reshape(16, NBAND)
    live = box_live.transpose(1, 2, 0).reshape(16, NBAND)
    shifts = box_shift.transpose(0, 1, 3, 2).reshape(2, 4)

    return call(
        main_kernel,
        (pltpu.VMEM((1, 8, NPIX), f32), pltpu.VMEM((CLASSES, 2, 2, 64), f32)),
        [ANY] * 15,
        (VMEM, VMEM),
        (
            pltpu.SMEM((32, NBAND), jnp.int32),
            pltpu.VMEM((16, NBAND), jnp.int32),
            pltpu.VMEM((16, NBAND), jnp.int32),
            pltpu.VMEM((4, 2, 8, 512), f32),
            pltpu.VMEM((2, 64, 512), f32),
            pltpu.VMEM((4, 2, 512), f32),
            pltpu.VMEM((2, 128, 128), f32),
            pltpu.VMEM((2, 64, 64), bf16),
            pltpu.VMEM((2, 512, 256), bf16),
            pltpu.VMEM((2, 256, 1024), bf16),
            pltpu.VMEM((2, 512, 256), bf16),
            pltpu.VMEM((2, 256, 256), bf16),
            pltpu.VMEM((2, 256, 256), bf16),
            pltpu.VMEM((16, 32, 256), bf16),
            pltpu.VMEM((32, 2, 4), jnp.int32),
            pltpu.SMEM((32, 2, 4), jnp.int32),
            pltpu.VMEM((2 * NQ, 2, 4), jnp.int32),
            pltpu.SMEM((2 * NQ, 2, 4), jnp.int32),
            pltpu.VMEM((32, REACH, 8, 128), bf16),
            pltpu.VMEM((32 * REACH, 8, 128), bf16),
            pltpu.VMEM((2, 256, 128), bf16),
            pltpu.VMEM((2, NQ, 32, 128), bf16),
            pltpu.VMEM((2, NQ, NZ, 2, 128), bf16),
            pltpu.VMEM((2, NQ, NZ, 2, 128), bf16),
            pltpu.VMEM((128, 8, 256), f32),
            pltpu.VMEM((25, NZ, 4, 128), bf16),
            pltpu.VMEM((25, NZ, 4, 128), bf16),
            pltpu.VMEM((NQ, 4, 4, 128), f32),
            pltpu.VMEM((32, 4, 4, 128), f32),
            pltpu.VMEM((4, 48, 64), f32),
            sems(6),
            sems(13),
            sems(11),
            sems(19),
        ),
        collective=0,
        name="main",
    )(
        micrograph, shifts, tops, classes, live, consts["row_twist"], consts["box_twist"], consts["box_quarter"], consts["col_twist"],
        consts["box_two"], consts["row_one"], consts["row_two"], consts["box_one"], consts["col_one"], consts["col_two"],
    )


def solution(mesh):
    in_specs = (P("rows", "half"), P(), P(), P(), P("rows", "half", None, None))
    out_specs = (P("half", "rows", None), P(None, None, "rows", "half"))
    return jax.shard_map(per_device, mesh=mesh, in_specs=in_specs, out_specs=out_specs, check_vma=False)
```

```python
import functools

import jax
import jax.numpy as jnp
import numpy as np
from jax import lax
from jax.experimental import pallas as pl
from jax.experimental.pallas import tpu as pltpu
from jax.sharding import PartitionSpec as P

BOX = 256
CLASSES = 50
NPIX = 4096
NZ, NQ, NY = 16, 8, 4
NBAND = 128
REACH = 9
MESH = pl.DeviceIdType.MESH
f32 = jnp.float32
bf16 = jnp.bfloat16
VMEM = pl.BlockSpec(memory_space=pltpu.VMEM)
SMEM = pl.BlockSpec(memory_space=pltpu.SMEM)
ANY = pl.BlockSpec(memory_space=pl.ANY)


def two_parts(matrix):
    high = matrix.astype(bf16)
    return np.stack([high, (matrix - high.astype(np.float64)).astype(bf16)])


def turn(left, right, length):
    angle = 2.0 * np.pi / length * np.mod(np.multiply.outer(left, right), length)
    return np.cos(angle), np.sin(angle)


@functools.lru_cache(None)
def tables():
    out = {}
    c, s = turn(np.arange(8), np.arange(8), 8)
    eye = np.eye(32)
    out["row_one"] = two_parts(np.concatenate([np.kron(c, eye), np.kron(-s, eye)]))
    angle = np.arange(8)[None] + 1024 * np.arange(4)[:, None]
    c, s = turn(angle, np.arange(512), NPIX)
    out["row_twist"] = np.stack([c, s], axis=1).astype(np.float32)
    c, s = turn(np.arange(128), np.arange(512), 512)
    real = np.concatenate([c, s], axis=1)
    imag = np.concatenate([-s, c], axis=1)
    both = np.stack([real, imag], axis=1).reshape(NZ, NQ, 2, 1024).transpose(1, 0, 2, 3)
    out["row_two"] = two_parts(both.reshape(256, 1024))
    c, s = turn(np.arange(128), np.arange(128), 128)
    real = np.stack([c, s], axis=2)
    imag = np.stack([-s, c], axis=2)
    both = np.concatenate([real, imag]).reshape(256, NZ, NQ, 2).transpose(0, 2, 1, 3)
    out["col_one"] = two_parts(both.reshape(256, 256))
    c, s = turn(np.arange(128), np.arange(32), NPIX)
    out["col_twist"] = np.stack([np.tile(c, (1, 4)), np.tile(s, (1, 4))]).astype(np.float32)
    c, s = turn(np.arange(32), np.arange(32), 32)
    same = np.eye(4)

    def spread(matrix):
        return np.einsum("tm,kl->tklm", matrix, same).reshape(128, 128)

    out["col_two"] = two_parts(np.block([[spread(c), spread(s)], [spread(-s), spread(c)]]))
    c, s = turn(np.arange(256), np.arange(256), 256)
    both = np.stack([c, -s]).reshape(2, NZ, NQ, 2, 256).transpose(2, 1, 0, 3, 4)
    out["box_one"] = two_parts(both.reshape(512, 256))
    c, s = turn(np.arange(32), np.arange(32), 32)
    out["box_two"] = two_parts(np.block([[c, s], [-s, c]]))
    lanes = np.concatenate([np.arange(384) // 48, (np.arange(128) >> 1) & 7])
    c, s = turn(np.arange(64), lanes, 256)
    out["box_twist"] = np.stack([c, s]).astype(np.float32)
    c, s = turn(np.arange(4), lanes, 4)
    out["box_quarter"] = np.stack([c, s], axis=1).reshape(4, 2, 512).astype(np.float32)
    return out


def halves(value):
    high = value.astype(bf16)
    return high, (value - high.astype(f32)).astype(bf16)


def mm(left, right):
    return lax.dot_general(left, right, (((1,), (0,)), ((), ())), preferred_element_type=f32)


def mmt(left, right):
    return lax.dot_general(left, right, (((1,), (1,)), ((), ())), preferred_element_type=f32)


def exact_product(table_ref, value, dot):
    return dot(table_ref[0], value) + dot(table_ref[1], value)


def full_product(table_ref, value, dot):
    high, low = halves(value)
    return dot(table_ref[0], high) + (dot(table_ref[1], high) + dot(table_ref[0], low))


def place():
    rows = lax.axis_index("rows")
    half = lax.axis_index("half")
    z = rows // NQ
    q = rows - z * NQ
    return rows, half, z, q, q * NY + half


def signal(barrier, rows, half):
    pl.semaphore_signal(barrier, inc=1, device_id=(rows, half), device_id_type=MESH)


def remote(src, dst, send, recv, rows, half):
    return pltpu.make_async_remote_copy(
        src_ref=src, dst_ref=dst, send_sem=send, recv_sem=recv, device_id=(rows, half), device_id_type=MESH
    )


def wait_for(ref, sem):
    pltpu.make_async_copy(ref, ref, sem).wait()


def loop(count, body, start=0, unroll=1):
    def step(index, carry):
        body(index)
        return carry

    lax.fori_loop(start, count, step, 0, unroll=unroll)


def signal_plane(barrier, z, p):
    def greet(k):
        other = lax.rem(p + k, 32)
        signal(barrier, z * NQ + other // NY, lax.rem(other, NY))

    loop(32, greet, 1)


def far_first(count):
    return sorted(range(1, count), key=lambda k: -min(k, count - k))


def main_kernel(
    mic_ref, shift_ref, tops_hbm, class_hbm, live_hbm, row_twist_hbm, box_twist_hbm, quarter_hbm, col_twist_hbm, box_two_hbm,
    row_one_hbm, row_two_hbm, box_one_hbm, col_one_hbm, col_two_hbm, power_ref, means_ref,
    tops_ref, class_ref, live_ref, row_twist_ref, box_twist_ref, quarter_ref, col_twist_ref, box_two_ref,
    row_one_ref, row_two_ref, box_one_ref, col_one_ref, col_two_ref, band_ref, table_in, table_ref, near_in, near_ref,
    boxes, boxes_in, freq, freq_mid, freq_ready, freq_in, held, to_z, landed, sums, got, early, local, load_sem, send, recv,
):
    rows, y, z, q, p = place()
    before, after = lax.rem(z + NZ - 1, NZ), lax.rem(z + 1, NZ)
    barrier = pltpu.get_barrier_semaphore()
    for k in far_first(NZ):
        signal(barrier, lax.rem(z + k, NZ) * NQ + q, y)
    loop(32, lambda k: signal(barrier, after * NQ + k // NY, lax.rem(k, NY)))
    loop(NQ, lambda k: signal(barrier, before * NQ + k, y))
    signal_plane(barrier, z, p)

    own = [
        pltpu.make_async_copy(shift_ref, table_in.at[p], local.at[4]),
        pltpu.make_async_copy(shift_ref, near_in.at[q], local.at[5]),
    ]
    for a in range(4):
        own.append(pltpu.make_async_copy(mic_ref.at[:, pl.ds(256 * a, 256)], band_ref.at[NY * y + a], local.at[a]))
    for copy in own:
        copy.start()
    loads = []
    for index, (source, target) in enumerate(
        (
            (tops_hbm, tops_ref),
            (row_twist_hbm, row_twist_ref),
            (row_one_hbm, row_one_ref),
            (row_two_hbm, row_two_ref),
            (class_hbm, class_ref),
            (live_hbm, live_ref),
            (box_one_hbm, box_one_ref),
            (quarter_hbm, quarter_ref),
            (box_twist_hbm, box_twist_ref),
            (col_twist_hbm, col_twist_ref),
            (col_one_hbm, col_one_ref),
            (col_two_hbm, col_two_ref),
            (box_two_hbm, box_two_ref),
        )
    ):
        loads.append(pltpu.make_async_copy(source, target, load_sem.at[index]))
        loads[-1].start()
    for copy in own:
        copy.wait()
    pl.semaphore_wait(barrier, 15 + 63 + NQ)

    mine = band_ref.at[pl.ds(NY * y, 4)]
    for k in (2, 1, 3):
        remote(mine, mine, send.at[6], recv.at[6], rows, lax.rem(y + k, NY)).start()
    for k in far_first(NQ):
        remote(
            near_in.at[q], near_in.at[q], send.at[10], recv.at[18], z * NQ + lax.rem(q + k, NQ), y
        ).start()
    for k in range(NQ):
        remote(near_in.at[q], near_in.at[NQ + q], send.at[10], recv.at[18], after * NQ + k, y).start()

    def tell(k):
        other = lax.rem(p + k, 32)
        remote(
            table_in.at[p], table_in.at[p], send.at[7], recv.at[7], z * NQ + other // NY, lax.rem(other, NY)
        ).start()

    loop(32, tell, 1)
    wait_for(near_in.at[pl.ds(0, 15)], recv.at[18])
    to_scalar = pltpu.make_async_copy(near_in, near_ref, local.at[0])
    to_scalar.start()
    wait_for(band_ref.at[pl.ds(0, 12)], recv.at[6])
    to_scalar.wait()
    loads[0].wait()

    lane = lax.broadcasted_iota(jnp.int32, (32, 256), 1)

    def one_band(d):
        near = q - d
        entry = jnp.where(near >= 0, near, 2 * NQ + near)
        home = lax.rem(rows - d + NBAND, NBAND)
        strips = []
        for s in range(4):
            left = tops_ref[(y * 4 + s) * 2 + 1, home] & 4095
            block = left >> 8
            offset = left & 255
            first = band_ref[block].astype(f32)
            second = band_ref[jnp.minimum(block + 1, 15)].astype(f32)
            picked = jnp.where(lane >= offset, first, second)
            shift = (near_ref[entry, 1, s] - offset) & 255
            strips.append(pltpu.roll(picked, shift, 1))
        boxes[:, d] = jnp.concatenate(strips, axis=0).T.reshape(32, 8, 128).astype(bf16)

    loop(REACH, one_band, unroll=9)

    here = p * REACH
    for level in range(NQ):

        @pl.when(q == level)
        def _():
            near, far = level + 1, REACH - 1 - level
            pltpu.make_async_copy(boxes.at[p, pl.ds(0, near)], boxes_in.at[pl.ds(here, near)], local.at[0]).start()
            for e in (0, 1, 3, 2):
                side = lax.rem(y + e, NY)
                group = (NY - e) % NY

                def send_both(k):
                    there = lax.rem(q + k, NQ)
                    target = there * NY + side
                    remote(
                        boxes.at[target, pl.ds(near, far)], boxes_in.at[pl.ds(here + near, far)],
                        send.at[2], recv.at[12 + group], before * NQ + there, side,
                    ).start()
                    remote(
                        boxes.at[target, pl.ds(0, near)], boxes_in.at[pl.ds(here, near)],
                        send.at[1], recv.at[8 + group], z * NQ + there, side,
                    ).start()

                def send_far_only(k):
                    there = lax.rem(q + k, NQ)
                    remote(
                        boxes.at[there * NY + side, pl.ds(near, far)], boxes_in.at[pl.ds(here + near, far)],
                        send.at[2], recv.at[12 + group], before * NQ + there, side,
                    ).start()

                loop(NQ, send_both, 1)
                if e == 0:
                    send_far_only(0)
                else:
                    send_both(0)

    for load in loads[1:4]:
        load.wait()
    real, imag = [], []
    cos_all, sin_all = row_twist_ref[y, 0], row_twist_ref[y, 1]
    for side in range(2):
        pixels = band_ref[:, :].reshape(8, 2, 32, 256)[:, side].reshape(256, 256)
        section = exact_product(row_one_ref, pixels, mm)
        cos = jnp.broadcast_to(cos_all[:, 256 * side : 256 * side + 256][:, None, :], (8, 32, 256)).reshape(256, 256)
        sin = jnp.broadcast_to(sin_all[:, 256 * side : 256 * side + 256][:, None, :], (8, 32, 256)).reshape(256, 256)
        real.append(section[:256] * cos + section[256:] * sin)
        imag.append(section[256:] * cos - section[:256] * sin)
    turned = jnp.concatenate(real + imag, axis=1)
    result = full_product(row_two_ref, turned, mmt).astype(bf16)
    freq[0] = result[:, :128]
    freq[1] = result[:, 128:]

    for k in far_first(NQ):
        other = lax.rem(q + k, NQ)
        remote(freq.at[:, pl.ds(32 * other, 32)], freq_mid.at[:, q], send.at[3], recv.at[3], z * NQ + other, y).start()
    own_mid = pltpu.make_async_copy(freq.at[:, pl.ds(32 * q, 32)], freq_mid.at[:, q], local.at[1])
    own_mid.start()
    own_mid.wait()
    wait_for(freq_mid.at[:, pl.ds(0, NQ - 1)], send.at[3])
    wait_for(freq_mid.at[:, pl.ds(0, NQ - 1)], recv.at[3])
    for h in range(2):
        freq_ready[h] = freq_mid[h].reshape(NQ, NZ, 2, 128)
    for k in far_first(NZ):
        other = lax.rem(z + k, NZ)
        remote(freq_ready.at[:, :, other], freq_in.at[:, :, z], send.at[4], recv.at[4], other * NQ + q, y).start()
    own_freq = pltpu.make_async_copy(freq_ready.at[:, :, z], freq_in.at[:, :, z], local.at[1])
    own_freq.start()

    wait_for(table_in.at[pl.ds(0, 31)], recv.at[7])
    to_scalar = pltpu.make_async_copy(table_in, table_ref, local.at[4])
    to_scalar.start()
    to_scalar.wait()

    lane = lax.broadcasted_iota(jnp.int32, (8, 128), 1)
    group = lane >> 5

    def one_home(q0, j):
        home = q0 * NY + j
        spun = []
        for d in range(REACH):
            piece = boxes_in[(((q0 + d) & 7) * NY + j) * REACH + d].astype(f32)
            spun.append([piece] + [pltpu.roll(piece, 32 * turns, 1) for turns in range(1, 4)])

        def joined(first, s):
            value = spun[first][(0 - s) % 4]
            for dd in range(1, 4):
                value = jnp.where(group == dd, spun[first + dd][(dd - s) % 4], value)
            return value

        for s in range(4):
            slot = home * 4 + s
            band = z * NQ + q0
            top = (tops_ref[(j * 4 + s) * 2, band] - band * 32) & 255
            shift = (table_ref[home, 0, s] - top) & 255
            low = jnp.where(lane >= top, joined(0, s), spun[8][(0 - s) % 4])
            held[slot] = pltpu.roll(jnp.concatenate([low, joined(4, s)], axis=1), shift, 1)

    for g in (0, 1, 3, 2):
        if g == 0:
            for level in range(NQ):

                @pl.when(q == level)
                def _():
                    wait_for(boxes_in.at[pl.ds(0, 36 - (level + 1))], recv.at[8])
                    wait_for(boxes_in.at[pl.ds(0, level + 1)], local.at[0])

        else:
            wait_for(boxes_in.at[pl.ds(0, 36)], recv.at[8 + g])
        wait_for(boxes_in.at[pl.ds(0, 36)], recv.at[12 + g])
        j = lax.rem(y + g, NY)
        loop(NQ, lambda q0: one_home(q0, j), unroll=2)

    for load in loads[4:7]:
        load.wait()
    labels = jnp.where(live_ref[...] == 1, class_ref[...], CLASSES)
    plane_labels = pltpu.roll(labels, lax.rem(NBAND - z * NQ, NBAND), 1)
    kind_lane = lax.broadcasted_iota(jnp.int32, (16, 128), 1)
    chosen = jnp.concatenate([(plane_labels[:, k : k + 1] == kind_lane).astype(f32) for k in range(NQ)], axis=0)
    chosen = chosen.T[:64].astype(bf16)
    columns = [mm(chosen, held[:, c, :].astype(bf16)) for c in range(8)]
    main = full_product(box_one_ref, jnp.concatenate([column[:48] for column in columns], axis=0), mmt)
    for t in range(2):
        for k in range(NQ):
            to_z[NQ * t + k] = main[64 * k : 64 * k + 64, 128 * t : 128 * t + 128].reshape(NZ, 4, 128).astype(bf16)
    for k in far_first(NZ):
        other = lax.rem(z + k, NZ)
        remote(
            to_z.at[pl.ds(0, 16), other], landed.at[pl.ds(0, 16), z], send.at[0], recv.at[0], other * NQ + q, y
        ).start()
    for k in range(NQ):
        to_z[2 * NQ + k] = main[64 * k : 64 * k + 64, 256:384].reshape(NZ, 4, 128).astype(bf16)
    rest = full_product(box_one_ref, jnp.concatenate([column[48:50] for column in columns], axis=0), mmt)
    rest = jnp.concatenate([rest[64 * k : 64 * k + 64] for k in range(NQ)], axis=1)
    to_z[24] = rest.reshape(NZ, 4, 128).astype(bf16)
    for k in far_first(NZ):
        other = lax.rem(z + k, NZ)
        remote(
            to_z.at[pl.ds(16, 9), other], landed.at[pl.ds(16, 9), z], send.at[8], recv.at[16], other * NQ + q, y
        ).start()
    own = pltpu.make_async_copy(to_z.at[:, z], landed.at[:, z], local.at[2])
    own.start()

    for load in loads[7:]:
        load.wait()
    cos_y, sin_y = quarter_ref[y, 0][None, :], quarter_ref[y, 1][None, :]
    cos = box_twist_ref[0] * cos_y - box_twist_ref[1] * sin_y
    sin = box_twist_ref[1] * cos_y + box_twist_ref[0] * sin_y

    kinds = lax.broadcasted_iota(jnp.int32, (64, 128), 0)
    counts = jnp.zeros((64, 128), f32)
    for k in range(16):
        counts = counts + (kinds == labels[k : k + 1, :]).astype(f32)
    inverse = 1.0 / (BOX * jnp.maximum(jnp.sum(counts, axis=1, keepdims=True), 1.0))

    own_freq.wait()
    wait_for(freq_in.at[:, :, pl.ds(0, NZ - 1)], send.at[4])
    wait_for(freq_in.at[:, :, pl.ds(0, NZ - 1)], recv.at[4])
    col_cos, col_sin = col_twist_ref[0], col_twist_ref[1]
    for h in range(2):
        section = exact_product(col_one_ref, freq_in[h].reshape(256, 128), mm)
        real = section[:128] * col_cos + section[128:] * col_sin
        imag = section[128:] * col_cos - section[:128] * col_sin
        result = full_product(col_two_ref, jnp.concatenate([real, imag], axis=1), mmt)
        power = (result[:128] * result[:128] + result[128:] * result[128:]) * (1.0 / (NPIX * NPIX))
        for tau in range(32):
            power_ref[0, 4 * h : 4 * h + 4, 128 * tau : 128 * tau + 128] = power[4 * tau : 4 * tau + 4]

    own.wait()
    mine = []
    for part, blocks in enumerate((pl.ds(0, 16), pl.ds(16, 9))):
        wait_for(landed.at[blocks, pl.ds(0, 15)], recv.at[16 * part])
        for t in ((0, 1), (2,))[part]:
            for k in range(NQ):
                sums[k, t] = jnp.sum(landed[NQ * t + k].astype(f32), axis=0)
        if part == 1:
            last = jnp.sum(landed[24].astype(f32), axis=0)
            for k in range(NQ):
                sums[k, 3] = last
        tiles = pl.ds(2 * part, 2)
        for k in far_first(32):
            other = lax.rem(p + k, 32)
            there = other // NY
            remote(
                sums.at[there, tiles], got.at[p, tiles], send.at[(5, 9)[part]], recv.at[(5, 17)[part]],
                z * NQ + there, lax.rem(other, NY),
            ).start()
        mine.append(pltpu.make_async_copy(sums.at[q, tiles], got.at[p, tiles], local.at[3 + part]))
        mine[-1].start()

    lanes = lax.broadcasted_iota(jnp.int32, (48, 384), 1)
    pick = (lax.rem(lanes, 48) == lax.broadcasted_iota(jnp.int32, (48, 384), 0)).astype(bf16)
    lanes = lax.broadcasted_iota(jnp.int32, (16, 128), 1)
    pick_rest = (((lanes >> 4) == q) & ((lanes & 1) == lax.broadcasted_iota(jnp.int32, (16, 128), 0))).astype(bf16)

    def turned_tiles(part):
        pieces = []
        for a in range(2):
            for t in (2 * part, 2 * part + 1):
                pieces.append(jnp.concatenate([got[:, t, a, :], got[:, t, 2 + a, :]], axis=0))
        section = full_product(box_two_ref, jnp.concatenate(pieces, axis=1), mm)
        at = slice(256 * part, 256 * part + 256)
        for a in range(2):
            real = jnp.concatenate([section[:32, 256 * a : 256 * a + 256]] * 2, axis=0)
            imag = jnp.concatenate([section[32:, 256 * a : 256 * a + 256]] * 2, axis=0)
            yield a, 0, halves(real * cos[:, at] + imag * sin[:, at])
            yield a, 1, halves(imag * cos[:, at] - real * sin[:, at])

    mine[0].wait()
    wait_for(got.at[pl.ds(0, 31), pl.ds(0, 2)], recv.at[5])
    for a, part, (high, low) in turned_tiles(0):
        early[2 * a + part] = mmt(pick[:, :256], high) + mmt(pick[:, :256], low)
    mine[1].wait()
    wait_for(got.at[pl.ds(0, 31), pl.ds(0, 2)], recv.at[17])
    for a, part, (high, low) in turned_tiles(1):
        total = mmt(pick[:, 256:], high[:, :128]) + mmt(pick[:, 256:], low[:, :128])
        means_ref[0:48, part, a, :] = (early[2 * a + part] + total) * inverse[:48]
        total = mmt(pick_rest, high[:, 128:]) + mmt(pick_rest, low[:, 128:])
        means_ref[48:50, part, a, :] = total[:2] * inverse[48:50]

    for level in range(NQ):

        @pl.when(q == level)
        def _():
            wait_for(boxes.at[pl.ds(0, 32), pl.ds(0, REACH - 1 - level)], send.at[2])
            wait_for(boxes.at[pl.ds(0, 31), pl.ds(0, level + 1)], send.at[1])

    wait_for(band_ref.at[pl.ds(0, 12)], send.at[6])
    wait_for(table_in.at[pl.ds(0, 31)], send.at[7])
    wait_for(near_in.at[pl.ds(0, 15)], send.at[10])
    wait_for(landed.at[pl.ds(0, 16), pl.ds(0, 15)], send.at[0])
    wait_for(landed.at[pl.ds(16, 9), pl.ds(0, 15)], send.at[8])
    wait_for(got.at[pl.ds(0, 31), pl.ds(0, 2)], send.at[5])
    wait_for(got.at[pl.ds(0, 31), pl.ds(0, 2)], send.at[9])


def call(kernel, outs, ins, out_specs, scratch=(), collective=None, name=None):
    params = dict(has_side_effects=True, collective_id=collective) if collective is not None else {}
    return pl.pallas_call(
        kernel,
        out_shape=outs,
        in_specs=ins,
        out_specs=out_specs,
        scratch_shapes=list(scratch),
        compiler_params=pltpu.CompilerParams(**params),
        name=name,
    )


def shape(*dims, dtype=bf16):
    return jax.ShapeDtypeStruct(dims, dtype)


def sems(count):
    return pltpu.SemaphoreType.DMA((count,))


def per_device(micrograph, box_tops, box_live, box_class, box_shift):
    consts = {name: jnp.asarray(value) for name, value in tables().items()}
    tops = box_tops.transpose(1, 2, 3, 0).reshape(32, NBAND)
    classes = box_class.transpose(1, 2, 0).reshape(16, NBAND)
    live = box_live.transpose(1, 2, 0).reshape(16, NBAND)
    shifts = box_shift.transpose(0, 1, 3, 2).reshape(2, 4)

    return call(
        main_kernel,
        (pltpu.VMEM((1, 8, NPIX), f32), pltpu.VMEM((CLASSES, 2, 2, 64), f32)),
        [ANY] * 15,
        (VMEM, VMEM),
        (
            pltpu.SMEM((32, NBAND), jnp.int32),
            pltpu.VMEM((16, NBAND), jnp.int32),
            pltpu.VMEM((16, NBAND), jnp.int32),
            pltpu.VMEM((4, 2, 8, 512), f32),
            pltpu.VMEM((2, 64, 512), f32),
            pltpu.VMEM((4, 2, 512), f32),
            pltpu.VMEM((2, 128, 128), f32),
            pltpu.VMEM((2, 64, 64), bf16),
            pltpu.VMEM((2, 512, 256), bf16),
            pltpu.VMEM((2, 256, 1024), bf16),
            pltpu.VMEM((2, 512, 256), bf16),
            pltpu.VMEM((2, 256, 256), bf16),
            pltpu.VMEM((2, 256, 256), bf16),
            pltpu.VMEM((16, 32, 256), bf16),
            pltpu.VMEM((32, 2, 4), jnp.int32),
            pltpu.SMEM((32, 2, 4), jnp.int32),
            pltpu.VMEM((2 * NQ, 2, 4), jnp.int32),
            pltpu.SMEM((2 * NQ, 2, 4), jnp.int32),
            pltpu.VMEM((32, REACH, 8, 128), bf16),
            pltpu.VMEM((32 * REACH, 8, 128), bf16),
            pltpu.VMEM((2, 256, 128), bf16),
            pltpu.VMEM((2, NQ, 32, 128), bf16),
            pltpu.VMEM((2, NQ, NZ, 2, 128), bf16),
            pltpu.VMEM((2, NQ, NZ, 2, 128), bf16),
            pltpu.VMEM((128, 8, 256), f32),
            pltpu.VMEM((25, NZ, 4, 128), bf16),
            pltpu.VMEM((25, NZ, 4, 128), bf16),
            pltpu.VMEM((NQ, 4, 4, 128), f32),
            pltpu.VMEM((32, 4, 4, 128), f32),
            pltpu.VMEM((4, 48, 64), f32),
            sems(6),
            sems(13),
            sems(11),
            sems(19),
        ),
        collective=0,
        name="main",
    )(
        micrograph, shifts, tops, classes, live, consts["row_twist"], consts["box_twist"], consts["box_quarter"], consts["col_twist"],
        consts["box_two"], consts["row_one"], consts["row_two"], consts["box_one"], consts["col_one"], consts["col_two"],
    )


def solution(mesh):
    in_specs = (P("rows", "half"), P(), P(), P(), P("rows", "half", None, None))
    out_specs = (P("half", "rows", None), P(None, None, "rows", "half"))
    return jax.shard_map(per_device, mesh=mesh, in_specs=in_specs, out_specs=out_specs, check_vma=False)
```
